256 devices in a mesh: seg: 8 (over y_hi, x), slab: 32 (over z, y_lo, core).
Axes of the slice: x: 4, y: 4 (y_hi: 2, y_lo: 2; y = y_hi * 2 + y_lo), z: 8, core: 2. Of those that a mesh axis runs over, the one named last changes fastest.
Arguments:
- states: float32 [8, 4, 256, 64, 128], P('seg', None, 'slab'), may hold values from -6 to 6
- viscosity: float32 [256, 64, 128], P('slab'), may hold values from 0.2 to 2
- inverse: float32 [4, 256, 256], replicated, may hold values from -0.375 to 0.375
Outputs:
- residual: float32 [8, 4, 256, 64, 128], P('seg', None, 'slab')
- gradient: float32 [8, 4, 256, 64, 128], P('seg', None, 'slab')
The draws below stay inside these ranges and needn't reach their ends.
All inputs are finite; a program needn't handle non-finite values.
Results may differ from the reference program's by a relative error of at most 0.000075.
Values sent between devices are 32-bit elements; how exact they have to be, the bound alone decides.
A program may use at most 128 MiB of HBM per device.

```python
import math
import jax
import jax.numpy as jnp
from jax import lax

NZ = 256
NY = 64
NX = 128
SEGS = 8


def level_of(key, dims, cuts, smallest, high):
    gain, own = 1.0, jax.random.fold_in(key, 6)
    for position, blocks in cuts:
        heights = jnp.exp(jax.random.uniform(jax.random.fold_in(own, position), (blocks,), jnp.float32, smallest / len(cuts), high / len(cuts)))
        gain = gain * jnp.repeat(heights, dims[position] // blocks).reshape([-1 if axis == position else 1 for axis in range(len(dims))])
    return gain


def scatter_about(own_key, extent, deviation, reach, split=(), held_as=jnp.bfloat16):
    gain = level_of(own_key, extent, split, -0.22, 0.18) if split else 1.0
    drawn = jax.random.normal(own_key, extent, jnp.float32) * deviation * gain
    return jnp.minimum(jnp.maximum(drawn, -reach), reach).astype(held_as)


def setup_inputs(seed: int = 0) -> dict:
    seeds = jax.random.split(jax.random.key(seed), 4)
    return {
        "states": scatter_about(seeds[0], (SEGS, 4, NZ, NY, NX), 1.0, 6.0, ((0, 8), (2, 32)), jnp.float32),
        "viscosity": jnp.clip(jnp.exp(math.log(2.0) - 2.3025851 * jax.random.uniform(seeds[1], (NZ, NY, NX), jnp.float32) ** level_of(seeds[1], (NZ, NY, NX), ((0, 32),), -0.2, 0.2)), 0.2, 2.0),
        "inverse": scatter_about(seeds[2], (4, NZ, NZ), NZ ** -0.5, 0.375, (), jnp.float32),
    }


time_step = 0.1
buoyancy = 1.0


def face_values(viscosity):
    viscous = viscosity[None]
    along_x = 0.5 * (viscous + jnp.roll(viscous, -1, axis=3))
    back_x = jnp.roll(along_x, 1, axis=3)
    along_y = 0.5 * (viscous + jnp.roll(viscous, -1, axis=2))
    back_y = 0.5 * (viscous + jnp.roll(viscous, 1, axis=2))
    return along_x, back_x, along_y, back_y


def horizontal(field_now, face_visc):
    along_x, back_x, along_y, back_y = face_visc
    north_side = jnp.roll(field_now, -1, axis=2)
    south_side = jnp.roll(field_now, 1, axis=2)
    east_side = jnp.roll(field_now, -1, axis=3)
    west_side = jnp.roll(field_now, 1, axis=3)
    return (along_x * (east_side - field_now) - back_x * (field_now - west_side)
            + along_y * (north_side - field_now) - back_y * (field_now - south_side))


def vertical(field_now):
    padded = jnp.pad(field_now, ((0, 0), (1, 1), (0, 0), (0, 0)))
    return padded[:, 2:] - padded[:, :-2]


def apply_columns(matrices, field_now):
    return jnp.einsum("fzk,fkyx->fzyx", matrices, field_now, precision=lax.Precision.HIGHEST)


def forcing(state_now):
    zero_plane = jnp.zeros_like(state_now[0])
    return jnp.stack([zero_plane, zero_plane, state_now[3], state_now[2]])


def advance(state_now, face_visc, matrices):
    slopes = vertical(state_now)
    explicit = state_now + time_step * (horizontal(state_now, face_visc) - state_now[2] * slopes + buoyancy * forcing(state_now))
    return apply_columns(matrices, explicit), slopes


def retreat(state_now, slopes, cotangent, face_visc, transposed):
    pulled = apply_columns(transposed, cotangent)
    scaled = time_step * pulled
    zero_plane = jnp.zeros_like(scaled[0])
    coupling = buoyancy * scaled[3] - jnp.sum(scaled * slopes, axis=0)
    coupled_terms = jnp.stack([zero_plane, zero_plane, coupling, buoyancy * scaled[2]])
    return pulled + horizontal(scaled, face_visc) + vertical(state_now[2] * scaled) + coupled_terms


def reference(states, viscosity, inverse):
    face_visc = face_values(viscosity)
    transposed = jnp.swapaxes(inverse, 1, 2)
    targets = jnp.roll(states, -1, axis=0)

    def forward_segment(pair):
        start_state, target = pair
        first_state = advance(start_state, face_visc, inverse)[0]
        second_state = advance(first_state, face_visc, inverse)[0]
        return second_state - target

    residual = lax.map(forward_segment, (states, targets))
    priors = jnp.roll(residual, 1, axis=0)

    def backward_segment(triple):
        start_state, residual_now, prior = triple
        first_state, slopes_start = advance(start_state, face_visc, inverse)
        slopes_first = vertical(first_state)
        carried = retreat(first_state, slopes_first, residual_now, face_visc, transposed)
        return retreat(start_state, slopes_start, carried, face_visc, transposed) - prior

    gradient = lax.map(backward_segment, (states, residual, priors))
    return residual, gradient
```

```python
import functools

import jax
import jax.numpy as jnp
from jax import lax
from jax.experimental import pallas as pl
from jax.experimental.pallas import tpu as pltpu
from jax.sharding import PartitionSpec as P

MESH = pl.DeviceIdType.MESH
NZ, NY, NX, NF = 256, 64, 128, 4
SLABS, PLANES, ROWS = 32, 8, 2
WIDE = ROWS * NX
PAD = 8
CHUNK = 32
DT = 0.1
GROUPS = ((2, 2), (0, 2))


def ring_of(slab, y_hi):
    z, yy, core = slab // 4, ((slab // 2) % 2 + y_hi) % 2, slab % 2
    chip = z + yy * (15 - 2 * z)
    return chip * 2 + core


def slab_of(ring, y_hi):
    chip, core = ring // 2, ring % 2
    yy = chip // 8
    z = chip + yy * (15 - 2 * chip)
    return z * 4 + ((yy + y_hi) % 2) * 2 + core


def partner(slab, k):
    z, y, core = slab // 4, (slab // 2) % 2, slab % 2
    j, i = k // 4, k % 4
    dz = 4 + (1 - 2 * (j % 2)) * ((j + 1) // 2)
    return ((z + dz) % 8) * 4 + ((y + 1 - i // 2) % 2) * 2 + (core + 1 - i % 2) % 2


def orbit_kernel(
    states, visc, inv, res_out, grad_out,
    send_q, send_v, q, first, adj1, adj2, target, prior, res, grad, vcol, faces, work, inv_t,
    halo, vhalo, recv_q, recv_v, recv_h, recv_vh, recv_t, recv_p, recv_r, recv_g,
    sem_q, sem_v, sem_h, sem_vh, sem_t, sem_p, sem_r, sem_g,
):
    seg, me = lax.axis_index("seg"), lax.axis_index("slab")
    y_hi = seg // 4
    ring = ring_of(me, y_hi)
    ahead, behind = (seg + 1) % 8, (seg + 7) % 8
    ahead_slab, behind_slab = slab_of(ring, ahead // 4), slab_of(ring, behind // 4)
    above, below = slab_of((ring + 1) % SLABS, y_hi), slab_of((ring + SLABS - 1) % SLABS, y_hi)

    barrier = pltpu.get_barrier_semaphore()

    def greet(k, carry):
        pl.semaphore_signal(
            barrier, inc=1, device_id=(seg, partner(me, k)), device_id_type=MESH
        )
        return carry

    lax.fori_loop(0, SLABS - 1, greet, 0)
    pl.semaphore_signal(barrier, inc=1, device_id=(ahead, ahead_slab), device_id_type=MESH)
    pl.semaphore_signal(barrier, inc=1, device_id=(behind, behind_slab), device_id_type=MESH)

    def pack(f):
        for y in range(NY):
            lanes = slice((y % 2) * NX, (y % 2 + 1) * NX)
            send_q[y // 2, f, :, lanes] = states[pl.ds(f * PLANES * NY + y, PLANES, stride=NY), :]

    for y in range(NY):
        lanes = slice((y % 2) * NX, (y % 2 + 1) * NX)
        send_v[y // 2, :, lanes] = visc[pl.ds(y, PLANES, stride=NY), :]
    for f in (2, 3):
        pack(f)
    pl.semaphore_wait(barrier, SLABS + 1)

    own = pl.ds(pl.multiple_of(PLANES * me, PLANES), PLANES)
    own_pad = pl.ds(pl.multiple_of(PLANES * me + PAD, PLANES), PLANES)

    def scatter_states(g):
        f0, n = GROUPS[g]

        def body(k, carry):
            to = partner(me, k)
            pltpu.make_async_remote_copy(
                send_q.at[ring_of(to, y_hi), pl.ds(f0, n)], q.at[pl.ds(f0, n), own_pad],
                sem_q.at[g], recv_q.at[g], device_id=(seg, to), device_id_type=MESH,
            ).start()
            return carry

        lax.fori_loop(0, SLABS - 1, body, 0)
        for f in range(f0, f0 + n):
            q[f, own_pad, :] = send_q[ring, f]

    def scatter_visc(k, carry):
        to = partner(me, k)
        pltpu.make_async_remote_copy(
            send_v.at[ring_of(to, y_hi)], vcol.at[own],
            sem_v, recv_v, device_id=(seg, to), device_id_type=MESH,
        ).start()
        return carry

    scatter_states(0)
    lax.fori_loop(0, SLABS - 1, scatter_visc, 0)
    vcol[own, :] = send_v[ring]
    for f in (0, 1):
        pack(f)
    scatter_states(1)

    edge = jnp.zeros((NF, PAD, WIDE), jnp.float32)
    for buf in (q, first, adj1, adj2):
        buf[:, 0:PAD, :] = edge
        buf[:, PAD + NZ : 2 * PAD + NZ, :] = edge
    for f in range(NF):
        inv_t[f] = inv[f].T

    some = pl.ds(0, PLANES * (SLABS - 1))

    def halo_copies(buf, phase, g):
        f0, n = GROUPS[g]
        fs, mid = pl.ds(f0, n), pl.ds(PAD, NZ)
        return (
            pltpu.make_async_remote_copy(
                buf.at[fs, mid, pl.ds(0, NX)], halo.at[phase, 1, fs],
                sem_h.at[phase, g, 0], recv_h.at[phase, g, 1],
                device_id=(seg, below), device_id_type=MESH,
            ),
            pltpu.make_async_remote_copy(
                buf.at[fs, mid, pl.ds(NX, NX)], halo.at[phase, 0, fs],
                sem_h.at[phase, g, 1], recv_h.at[phase, g, 0],
                device_id=(seg, above), device_id_type=MESH,
            ),
        )

    visc_copies = (
        pltpu.make_async_remote_copy(
            vcol.at[:, pl.ds(0, NX)], vhalo.at[1], sem_vh.at[0], recv_vh.at[1],
            device_id=(seg, below), device_id_type=MESH,
        ),
        pltpu.make_async_remote_copy(
            vcol.at[:, pl.ds(NX, NX)], vhalo.at[0], sem_vh.at[1], recv_vh.at[0],
            device_id=(seg, above), device_id_type=MESH,
        ),
    )

    def target_copy(g):
        f0, n = GROUPS[g]
        fs = pl.ds(f0, n)
        return pltpu.make_async_remote_copy(
            q.at[fs, pl.ds(PAD, NZ)], target.at[fs], sem_t.at[g], recv_t.at[g],
            device_id=(behind, behind_slab), device_id_type=MESH,
        )

    def prior_copy(g):
        f0, n = GROUPS[g]
        fs = pl.ds(f0, n)
        return pltpu.make_async_remote_copy(
            res.at[fs], prior.at[fs], sem_p.at[g], recv_p.at[g],
            device_id=(ahead, ahead_slab), device_id_type=MESH,
        )

    def wait_halo(buf, phase, g):
        for copy in halo_copies(buf, phase, g):
            copy.wait_recv()

    def start_halo(buf, phase, g):
        for copy in halo_copies(buf, phase, g):
            copy.start()

    def scatter_back(src, dst, sem, recv, g):
        f0, n = GROUPS[g]
        fs = pl.ds(f0, n)

        def body(k, carry):
            to = partner(me, k)
            pltpu.make_async_remote_copy(
                src.at[fs, :, pl.ds(pl.multiple_of(PLANES * to, PLANES), PLANES)],
                dst.at[ring, fs], sem.at[g], recv.at[g],
                device_id=(seg, to), device_id_type=MESH,
            ).start()
            return carry

        lax.fori_loop(0, SLABS - 1, body, 0)
        for f in range(f0, f0 + n):
            dst[ring, f] = src[f, :, own, :]

    def wait_many(ref, sem):
        pltpu.make_async_copy(ref, ref, sem).wait()

    def lanes_of(row):
        return slice(row * NX, (row + 1) * NX)

    def over_chunks(body):
        def step(k, carry):
            body(pl.multiple_of(k * CHUNK, CHUNK))
            return carry

        lax.fori_loop(0, NZ // CHUNK, step, 0)

    def face_values():
        def body(z0):
            zs = pl.ds(z0, CHUNK)
            for row in range(ROWS):
                ln = lanes_of(row)
                v, o = vcol[zs, ln], vcol[zs, lanes_of(1 - row)]
                north = o if row == 0 else vhalo[1, zs, :]
                south = vhalo[0, zs, :] if row == 0 else o
                faces[0, zs, ln] = 0.5 * (v + pltpu.roll(v, NX - 1, 1))
                faces[1, zs, ln] = 0.5 * (pltpu.roll(v, 1, 1) + v)
                faces[2, zs, ln] = 0.5 * (v + north)
                faces[3, zs, ln] = 0.5 * (v + south)

        over_chunks(body)

    def horizontal(buf, phase, f, row, z0, v):
        zs, ln = pl.ds(z0, CHUNK), lanes_of(row)
        o = buf[f, pl.ds(z0 + PAD, CHUNK), lanes_of(1 - row)]
        north = o if row == 0 else halo[phase, 1, f, zs, :]
        south = halo[phase, 0, f, zs, :] if row == 0 else o
        return (
            faces[0, zs, ln] * (pltpu.roll(v, NX - 1, 1) - v)
            - faces[1, zs, ln] * (v - pltpu.roll(v, 1, 1))
            + faces[2, zs, ln] * (north - v)
            - faces[3, zs, ln] * (v - south)
        )

    def window(buf, f, row, z0):
        return buf[f, pl.ds(z0, CHUNK + 2 * PAD), lanes_of(row)]

    def middle(win):
        return win[PAD : PAD + CHUNK]

    def slope(win):
        return win[PAD + 1 : PAD + 1 + CHUNK] - win[PAD - 1 : PAD - 1 + CHUNK]

    def explicit(buf, phase, f):
        def body(z0):
            for row in range(ROWS):
                win = window(buf, f, row, z0)
                v = middle(win)
                mid = pl.ds(z0 + PAD, CHUNK)
                term = horizontal(buf, phase, f, row, z0, v) - buf[2, mid, lanes_of(row)] * slope(win)
                if f >= 2:
                    term = term + buf[5 - f, mid, lanes_of(row)]
                work[pl.ds(z0, CHUNK), lanes_of(row)] = v + DT * term

        over_chunks(body)

    def adjoint(state, buf, phase, f, minus=None, into=None):
        def body(z0):
            for row in range(ROWS):
                ln, zs, mid = lanes_of(row), pl.ds(z0, CHUNK), pl.ds(z0 + PAD, CHUNK)
                win = window(buf, f, row, z0)
                v = middle(win)
                term = horizontal(buf, phase, f, row, z0, v) + slope(window(state, 2, row, z0) * win)
                if f >= 2:
                    term = term + buf[5 - f, mid, ln]
                if f == 2:
                    total = None
                    for g in range(NF):
                        part = buf[g, mid, ln] * slope(window(state, g, row, z0))
                        total = part if total is None else total + part
                    term = term - total
                out = v + DT * term
                if minus is None:
                    work[zs, ln] = out
                else:
                    into[f, row, zs, :] = out - minus[f, row, zs, :]

        over_chunks(body)

    def product(matrix, rhs):
        return jnp.dot(
            matrix, rhs, precision=lax.Precision.HIGHEST, preferred_element_type=jnp.float32
        )

    wait_many(q.at[pl.ds(2, 2), some], recv_q.at[0])
    start_halo(q, 0, 0)
    target_copy(0).start()
    wait_many(vcol.at[some], recv_v)
    for copy in visc_copies:
        copy.start()
    for copy in visc_copies:
        copy.wait_recv()
    face_values()

    order = ((2, 3), (0, 1))
    for g in range(2):
        if g == 1:
            wait_many(q.at[pl.ds(0, 2), some], recv_q.at[1])
            start_halo(q, 0, 1)
            target_copy(1).start()
        wait_halo(q, 0, g)
        for f in order[g]:
            explicit(q, 0, f)
            first[f, pl.ds(PAD, NZ), :] = product(inv[f], work[...])
        start_halo(first, 1, g)

    for g in range(2):
        wait_halo(first, 1, g)
        target_copy(g).wait_recv()
        for f in order[g]:
            explicit(first, 1, f)
            end = product(inv[f], work[...]) - target[f]
            for row in range(ROWS):
                res[f, row] = end[:, lanes_of(row)]
            adj1[f, pl.ds(PAD, NZ), :] = product(inv_t[f], end)
        start_halo(adj1, 2, g)
        prior_copy(g).start()
        scatter_back(res, res_out, sem_r, recv_r, g)

    for g in range(2):
        wait_halo(adj1, 2, g)
        for f in order[g]:
            adjoint(first, adj1, 2, f)
            adj2[f, pl.ds(PAD, NZ), :] = product(inv_t[f], work[...])
        start_halo(adj2, 3, g)

    for g in range(2):
        wait_halo(adj2, 3, g)
        prior_copy(g).wait_recv()
        for f in order[g]:
            adjoint(q, adj2, 3, f, minus=prior, into=grad)
        scatter_back(grad, grad_out, sem_g, recv_g, g)

    wait_many(vcol.at[some], sem_v)
    for copy in visc_copies:
        copy.wait_send()
    for g in range(2):
        fs = pl.ds(GROUPS[g][0], GROUPS[g][1])
        wait_many(q.at[fs, some], sem_q.at[g])
        for phase, buf in enumerate((q, first, adj1, adj2)):
            for copy in halo_copies(buf, phase, g):
                copy.wait_send()
        target_copy(g).wait_send()
        prior_copy(g).wait_send()
        for sem in (recv_r, recv_g, sem_r, sem_g):
            wait_many(res.at[fs, :, some], sem.at[g])


def finish_kernel(res_in, grad_in, res_out, grad_out):
    for src, dst in ((res_in, res_out), (grad_in, grad_out)):
        for plane in range(NF * PLANES):
            for block in range(4):
                for row in range(ROWS):
                    dst[pl.ds(plane * NY + block * 16 + row, 8, stride=2), :] = src[
                        pl.ds(
                            block * 8 * NF * ROWS * PLANES + (plane // PLANES * ROWS + row) * PLANES + plane % PLANES,
                            8, stride=NF * ROWS * PLANES,
                        ),
                        :,
                    ]


def local(states, viscosity, inverse):
    vmem = pl.BlockSpec(memory_space=pltpu.VMEM)
    f32 = jnp.float32
    sem = pltpu.SemaphoreType.DMA
    back = jax.ShapeDtypeStruct((SLABS, NF, ROWS, PLANES, NX), f32)
    padded = pltpu.VMEM((NF, NZ + 2 * PAD, WIDE), f32)
    column = pltpu.VMEM((NF, NZ, WIDE), f32)
    rows = pltpu.VMEM((NF, ROWS, NZ, NX), f32)
    res, grad = pl.pallas_call(
        orbit_kernel,
        out_shape=(back, back),
        in_specs=[vmem] * 3,
        out_specs=(vmem, vmem),
        scratch_shapes=[
            pltpu.VMEM((SLABS, NF, PLANES, WIDE), f32),
            pltpu.VMEM((SLABS, PLANES, WIDE), f32),
            padded, padded, padded, padded,
            column, rows, rows, rows,
            pltpu.VMEM((NZ, WIDE), f32),
            pltpu.VMEM((4, NZ, WIDE), f32),
            pltpu.VMEM((NZ, WIDE), f32),
            column,
            pltpu.VMEM((4, 2, NF, NZ, NX), f32),
            pltpu.VMEM((2, NZ, NX), f32),
            sem((2,)), sem, sem((4, 2, 2)), sem((2,)), sem((2,)), sem((2,)), sem((2,)), sem((2,)),
            sem((2,)), sem, sem((4, 2, 2)), sem((2,)), sem((2,)), sem((2,)), sem((2,)), sem((2,)),
        ],
        compiler_params=pltpu.CompilerParams(
            collective_id=0, has_side_effects=True, vmem_limit_bytes=48 << 20
        ),
        name="orbit",
    )(
        states.reshape(NF * PLANES * NY, NX),
        viscosity.reshape(PLANES * NY, NX),
        inverse,
    )
    flat = jax.ShapeDtypeStruct((NF * PLANES * NY, NX), f32)
    res, grad = pl.pallas_call(
        finish_kernel,
        out_shape=(flat, flat),
        in_specs=[vmem] * 2,
        out_specs=(vmem, vmem),
        compiler_params=pltpu.CompilerParams(vmem_limit_bytes=16 << 20),
        name="finish",
    )(res.reshape(-1, NX), grad.reshape(-1, NX))
    shape = (1, NF, PLANES, NY, NX)
    return res.reshape(shape), grad.reshape(shape)


def solution(mesh):
    spec = P("seg", None, "slab", None, None)
    return jax.shard_map(
        local,
        mesh=mesh,
        in_specs=(spec, P("slab", None, None), P()),
        out_specs=(spec, spec),
        check_vma=False,
    )
```

```python
import jax
import jax.numpy as jnp
from jax import lax
from jax.experimental import pallas as pl
from jax.experimental.pallas import tpu as pltpu
from jax.sharding import PartitionSpec as P

MESH = pl.DeviceIdType.MESH
NZ, NY, NX, NF = 256, 64, 128, 4
SLABS, PLANES = 32, 8
PAD = 8
CHUNK = 64
BLOCKS = CHUNK // 8
CHUNKS = NZ // CHUNK
SIDE = 16
DT = 0.1
GROUPS = ((2, 2), (0, 2))
EAST, WEST, NORTH, SOUTH = range(4)


def patch_of(slab, y_hi):
    return slab // 4, 2 * (((slab // 2) % 2 + y_hi) % 2) + slab % 2


def slab_of(z, quarter, y_hi):
    return z * 4 + ((quarter // 2 + y_hi) % 2) * 2 + quarter % 2


def partner(slab, k):
    z, y, core = slab // 4, (slab // 2) % 2, slab % 2
    j, i = k // 4, k % 4
    dz = 4 + (1 - 2 * (j % 2)) * ((j + 1) // 2)
    return ((z + dz) % 8) * 4 + ((y + 1 - i // 2) % 2) * 2 + (core + 1 - i % 2) % 2


def lane_index(rows):
    return lax.broadcasted_iota(jnp.int32, (rows, NX), 1)


def roll(value, shift):
    shift = shift % NX
    return value if shift == 0 else pltpu.roll(value, shift, 1)


def swap_blocks(tiles):
    tiles, lane = list(tiles), lane_index(8)
    for bit in (1, 2, 4):
        low = (lane & (SIDE * bit)) == 0
        for i in range(8):
            if not i & bit:
                a, b = tiles[i], tiles[i | bit]
                tiles[i] = jnp.where(low, a, roll(b, SIDE * bit))
                tiles[i | bit] = jnp.where(low, roll(a, -SIDE * bit), b)
    return tiles


def pack_sides(tile_of):
    lane = lane_index(8)
    east = west = north = south = jnp.zeros((8, NX), jnp.float32)
    for b in range(BLOCKS):
        for j in range(2):
            tile, i = tile_of(b, j), 2 * b + j
            here = lane % SIDE == i
            east = jnp.where(here, roll(tile, i), east)
            west = jnp.where(here, roll(tile, i - SIDE + 1), west)
            block = lane // SIDE == b
            if j == 0:
                north = jnp.where(block, roll(tile, SIDE * b), north)
            else:
                south = jnp.where(block, roll(tile, SIDE * b - NX + SIDE), south)
    return east, west, north, south


def neighbours(halves, sides):
    lane = lane_index(CHUNK)
    last, start = lane % SIDE == SIDE - 1, lane % SIDE == 0
    up = [roll(v, -SIDE) for v in halves]
    down = [roll(v, SIDE) for v in halves]

    def spread(side, shift_of):
        return jnp.concatenate([roll(sides[side], shift_of(b)) for b in range(BLOCKS)], axis=0)

    up.append(spread(NORTH, lambda b: NX - SIDE - SIDE * b))
    down.insert(0, spread(SOUTH, lambda b: -SIDE * b))
    found = []
    for j, v in enumerate(halves):
        east = jnp.where(last, spread(EAST, lambda b: SIDE - 1 - 2 * b - j), roll(v, -1))
        west = jnp.where(start, spread(WEST, lambda b: -2 * b - j), roll(v, 1))
        north = jnp.where(lane < NX - SIDE, up[j], up[j + 1])
        south = jnp.where(lane < SIDE, down[j], down[j + 1])
        found.append((east, west, north, south))
    return found


def orbit_kernel(
    states_hbm, visc_hbm, inv_hbm, res_out, grad_out,
    states, visc, inv, send_q, send_v, q, first, adj1, adj2, target, prior, res, grad,
    vset, vcol, faces, work, inv_t, side, halo, vside, vhalo,
    sem_in, recv_q, recv_v, recv_vx, recv_h, recv_vh, recv_t, recv_p, recv_r, recv_g,
    sem_q, sem_v, sem_vx, sem_h, sem_vh, sem_t, sem_p, sem_r, sem_g,
):
    seg, me = lax.axis_index("seg"), lax.axis_index("slab")
    y_hi, x = seg // 4, seg % 4
    z, quarter = patch_of(me, y_hi)
    ahead, behind = (seg + 1) % 8, (seg + 7) % 8
    ahead_slab, behind_slab = slab_of(z, quarter, ahead // 4), slab_of(z, quarter, behind // 4)
    giver = me % 2 + 2 * ((z + (me // 2) % 2) % 2) == x
    takers = (
        (me + SLABS - 4) % SLABS,
        (me + 4) % SLABS,
        slab_of(z, (quarter + 3) % 4, y_hi),
        slab_of(z, (quarter + 1) % 4, y_hi),
    )

    half = NF * PLANES * NY // 2
    loads = (
        pltpu.make_async_copy(states_hbm.at[pl.ds(half, half)], states.at[pl.ds(half, half)], sem_in.at[0]),
        pltpu.make_async_copy(visc_hbm, visc, sem_in.at[1]),
        pltpu.make_async_copy(states_hbm.at[pl.ds(0, half)], states.at[pl.ds(0, half)], sem_in.at[2]),
        pltpu.make_async_copy(inv_hbm, inv, sem_in.at[3]),
    )
    for load in loads:
        load.start()

    barrier = pltpu.get_barrier_semaphore()

    def greet(k, carry):
        pl.semaphore_signal(
            barrier, inc=1, device_id=(seg, partner(me, k)), device_id_type=MESH
        )
        return carry

    lax.fori_loop(0, SLABS - 1, greet, 0)
    pl.semaphore_signal(barrier, inc=1, device_id=(ahead, ahead_slab), device_id_type=MESH)
    pl.semaphore_signal(barrier, inc=1, device_id=(behind, behind_slab), device_id_type=MESH)
    for d in (1, 2, 3):
        pl.semaphore_signal(
            barrier, inc=1, device_id=(y_hi * 4 + (x + d) % 4, me), device_id_type=MESH
        )

    def rows_of(f, y):
        return pl.ds(f * PLANES * NY + y, PLANES, stride=NY)

    def pack(f):
        for block in range(NY // 8):
            tiles = swap_blocks([states[rows_of(f, 8 * block + i), :] for i in range(8)])
            for i in range(8):
                send_q[i, block // 2, f, block % 2] = tiles[i]

    loads[0].wait()
    for f in (2, 3):
        pack(f)
    pl.semaphore_wait(barrier, SLABS + 4)

    own = pl.ds(pl.multiple_of(PLANES * me, PLANES), PLANES)
    own_pad = pl.ds(pl.multiple_of(PLANES * me + PAD, PLANES), PLANES)

    def scatter_states(g):
        f0, n = GROUPS[g]

        def body(k, carry):
            to = partner(me, k)
            zt, qt = patch_of(to, y_hi)
            pltpu.make_async_remote_copy(
                send_q.at[zt, qt, pl.ds(f0, n)], q.at[pl.ds(f0, n), :, own_pad],
                sem_q.at[g], recv_q.at[g], device_id=(seg, to), device_id_type=MESH,
            ).start()
            return carry

        lax.fori_loop(0, SLABS - 1, body, 0)
        for f in range(f0, f0 + n):
            q[f, :, own_pad, :] = send_q[z, quarter, f]

    def wait_many(ref, sem):
        pltpu.make_async_copy(ref, ref, sem).wait()

    scatter_states(0)
    loads[1].wait()

    @pl.when(giver)
    def _():
        for block in range(NY // 8):
            tiles = swap_blocks([visc[rows_of(0, 8 * block + i), :] for i in range(8)])
            for i in range(8):
                send_v[i, block // 2, block % 2] = tiles[i]

        def body(k, carry):
            to = partner(me, k)
            zt, qt = patch_of(to, y_hi)
            pltpu.make_async_remote_copy(
                send_v.at[zt, qt], vset.at[x, z],
                sem_v, recv_v, device_id=(seg, to), device_id_type=MESH,
            ).start()
            return carry

        lax.fori_loop(0, SLABS - 1, body, 0)
        vset[x, z] = send_v[z, quarter]

    loads[2].wait()
    for f in (0, 1):
        pack(f)
    scatter_states(1)

    edge = jnp.zeros((NF, 2, PAD, NX), jnp.float32)
    for buf in (q, first, adj1, adj2):
        buf[:, :, 0:PAD, :] = edge
        buf[:, :, PAD + NZ : 2 * PAD + NZ, :] = edge

    @pl.when(giver)
    def _():
        wait_many(vset.at[x, pl.ds(0, 7)], recv_v)

    @pl.when(jnp.logical_not(giver))
    def _():
        wait_many(vset.at[x, pl.ds(0, 8)], recv_v)

    shares = [
        pltpu.make_async_remote_copy(
            vset.at[x], vset.at[x], sem_vx.at[d - 1], recv_vx.at[d - 1],
            device_id=(y_hi * 4 + (x + d) % 4, me), device_id_type=MESH,
        )
        for d in (1, 2, 3)
    ]
    for share in shares:
        share.start()
    loads[3].wait()
    for f in range(NF):
        inv_t[f] = inv[f].T
    for share in shares:
        share.wait_recv()
    for xs in range(4):
        for zs in range(8):
            plane = PLANES * (zs * 4 + ((xs // 2 + zs) % 2) * 2 + xs % 2)
            for j in range(2):
                vcol[j, plane : plane + PLANES, :] = vset[xs, zs, j]

    def over_chunks(body):
        def step(k, carry):
            body(k)
            return carry

        lax.fori_loop(0, CHUNKS, step, 0)

    def at(k, pad=0):
        return pl.ds(pl.multiple_of(k * CHUNK + pad, 8), CHUNK)

    def packed(k):
        return pl.ds(pl.multiple_of(k * 8, 8), 8)

    def visc_copies():
        return [
            pltpu.make_async_remote_copy(
                vside.at[d], vhalo.at[d], sem_vh.at[d], recv_vh.at[d],
                device_id=(seg, takers[d]), device_id_type=MESH,
            )
            for d in range(4)
        ]

    def pack_visc(k):
        sides = pack_sides(lambda b, j: vcol[j, pl.ds(pl.multiple_of(k * CHUNK + 8 * b, 8), 8), :])
        for d in range(4):
            vside[d, packed(k), :] = sides[d]

    over_chunks(pack_visc)
    for copy in visc_copies():
        copy.start()

    def halo_copies(phase, g):
        f0, n = GROUPS[g]
        fs = pl.ds(f0, n)
        return [
            pltpu.make_async_remote_copy(
                side.at[phase, d, fs], halo.at[phase, d, fs],
                sem_h.at[phase, g, d], recv_h.at[phase, g, d],
                device_id=(seg, takers[d]), device_id_type=MESH,
            )
            for d in range(4)
        ]

    def start_halo(buf, phase, g):
        f0, n = GROUPS[g]

        def body(k):
            for f in range(f0, f0 + n):
                sides = pack_sides(
                    lambda b, j: buf[f, j, pl.ds(pl.multiple_of(k * CHUNK + 8 * b + PAD, 8), 8), :]
                )
                for d in range(4):
                    side[phase, d, f, packed(k), :] = sides[d]

        over_chunks(body)
        for copy in halo_copies(phase, g):
            copy.start()

    def wait_halo(phase, g):
        for copy in halo_copies(phase, g):
            copy.wait_recv()

    def target_copy(g):
        f0, n = GROUPS[g]
        fs = pl.ds(f0, n)
        return pltpu.make_async_remote_copy(
            q.at[fs, :, pl.ds(PAD, NZ)], target.at[fs], sem_t.at[g], recv_t.at[g],
            device_id=(behind, behind_slab), device_id_type=MESH,
        )

    def prior_copy(g):
        f0, n = GROUPS[g]
        fs = pl.ds(f0, n)
        return pltpu.make_async_remote_copy(
            res.at[fs], prior.at[fs], sem_p.at[g], recv_p.at[g],
            device_id=(ahead, ahead_slab), device_id_type=MESH,
        )

    def scatter_back(src, dst, sem, recv, g):
        f0, n = GROUPS[g]
        fs = pl.ds(f0, n)

        def body(k, carry):
            to = partner(me, k)
            pltpu.make_async_remote_copy(
                src.at[fs, :, pl.ds(pl.multiple_of(PLANES * to, PLANES), PLANES)],
                dst.at[z, quarter, fs], sem.at[g], recv.at[g],
                device_id=(seg, to), device_id_type=MESH,
            ).start()
            return carry

        lax.fori_loop(0, SLABS - 1, body, 0)
        for f in range(f0, f0 + n):
            dst[z, quarter, f] = src[f, :, own, :]

    def face_values(k):
        halves = [vcol[j, at(k), :] for j in range(2)]
        found = neighbours(halves, [vhalo[d, packed(k), :] for d in range(4)])
        for j in range(2):
            for d in range(4):
                faces[d, j, at(k), :] = 0.5 * (halves[j] + found[j][d])

    def horizontal(buf, phase, f, k, halves):
        found = neighbours(halves, [halo[phase, d, f, packed(k), :] for d in range(4)])
        terms = []
        for j in range(2):
            v, (east, west, north, south) = halves[j], found[j]
            terms.append(
                faces[EAST, j, at(k), :] * (east - v)
                - faces[WEST, j, at(k), :] * (v - west)
                + faces[NORTH, j, at(k), :] * (north - v)
                - faces[SOUTH, j, at(k), :] * (v - south)
            )
        return terms

    def window(buf, f, j, k):
        return buf[f, j, pl.ds(pl.multiple_of(k * CHUNK, 8), CHUNK + 2 * PAD), :]

    def middle(win):
        return win[PAD : PAD + CHUNK]

    def slope(win):
        return win[PAD + 1 : PAD + 1 + CHUNK] - win[PAD - 1 : PAD - 1 + CHUNK]

    def lanes_of(j):
        return slice(j * NX, (j + 1) * NX)

    def explicit(buf, phase, f):
        def body(k):
            wins = [window(buf, f, j, k) for j in range(2)]
            halves = [middle(win) for win in wins]
            terms = horizontal(buf, phase, f, k, halves)
            for j in range(2):
                term = terms[j] - buf[2, j, at(k, PAD), :] * slope(wins[j])
                if f >= 2:
                    term = term + buf[5 - f, j, at(k, PAD), :]
                work[at(k), lanes_of(j)] = halves[j] + DT * term

        over_chunks(body)

    def adjoint(state, buf, phase, f, minus=None, into=None):
        def body(k):
            wins = [window(buf, f, j, k) for j in range(2)]
            halves = [middle(win) for win in wins]
            terms = horizontal(buf, phase, f, k, halves)
            for j in range(2):
                term = terms[j] + slope(window(state, 2, j, k) * wins[j])
                if f >= 2:
                    term = term + buf[5 - f, j, at(k, PAD), :]
                if f == 2:
                    total = None
                    for g in range(NF):
                        part = buf[g, j, at(k, PAD), :] * slope(window(state, g, j, k))
                        total = part if total is None else total + part
                    term = term - total
                out = halves[j] + DT * term
                if minus is None:
                    work[at(k), lanes_of(j)] = out
                else:
                    into[f, j, at(k), :] = out - minus[f, j, at(k), :]

        over_chunks(body)

    def product(matrix):
        return jnp.dot(
            matrix, work[...], precision=lax.Precision.HIGHEST, preferred_element_type=jnp.float32
        )

    def store(buf, f, value):
        for j in range(2):
            buf[f, j, PAD : PAD + NZ, :] = value[:, lanes_of(j)]

    def forward(g):
        f0, n = GROUPS[g]
        wait_halo(0, g)
        for f in range(f0, f0 + n):
            explicit(q, 0, f)
            store(first, f, product(inv[f]))
        start_halo(first, 1, g)
        wait_halo(1, g)
        target_copy(g).wait_recv()
        for f in range(f0, f0 + n):
            explicit(first, 1, f)
            end = product(inv[f])
            for j in range(2):
                gap = end[:, lanes_of(j)] - target[f, j]
                res[f, j] = gap
                work[:, lanes_of(j)] = gap
            store(adj1, f, product(inv_t[f]))
        start_halo(adj1, 2, g)
        prior_copy(g).start()
        scatter_back(res, res_out, sem_r, recv_r, g)

    def backward(g):
        f0, n = GROUPS[g]
        wait_halo(2, g)
        for f in range(f0, f0 + n):
            adjoint(first, adj1, 2, f)
            store(adj2, f, product(inv_t[f]))
        start_halo(adj2, 3, g)

    def closing(g):
        f0, n = GROUPS[g]
        wait_halo(3, g)
        prior_copy(g).wait_recv()
        for f in range(f0, f0 + n):
            adjoint(q, adj2, 3, f, minus=prior, into=grad)
        scatter_back(grad, grad_out, sem_g, recv_g, g)

    def arrive(g):
        f0, n = GROUPS[g]
        wait_many(q.at[pl.ds(f0, n), :, some], recv_q.at[g])
        start_halo(q, 0, g)
        target_copy(g).start()

    some = pl.ds(0, PLANES * (SLABS - 1))
    arrive(0)
    for copy in visc_copies():
        copy.wait_recv()
    over_chunks(face_values)
    forward(0)
    arrive(1)
    forward(1)
    backward(0)
    backward(1)
    closing(0)
    closing(1)

    @pl.when(giver)
    def _():
        wait_many(send_v.at[pl.ds(0, 7)], sem_v)
        wait_many(send_v.at[0, pl.ds(0, 3)], sem_v)

    for copy in shares + visc_copies():
        copy.wait_send()
    for g in range(2):
        fs = pl.ds(GROUPS[g][0], GROUPS[g][1])
        wait_many(q.at[fs, :, some], sem_q.at[g])
        for phase in range(4):
            for copy in halo_copies(phase, g):
                copy.wait_send()
        target_copy(g).wait_send()
        prior_copy(g).wait_send()
        for sem in (recv_r, recv_g, sem_r, sem_g):
            wait_many(res.at[fs, :, some], sem.at[g])


def finish_kernel(res_in, grad_in, res_out, grad_out):
    for src, dst in ((res_in, res_out), (grad_in, grad_out)):
        for f in range(NF):
            for block in range(NY // 8):
                tiles = swap_blocks(
                    [
                        src[pl.ds((((i * 4 + block // 2) * NF + f) * 2 + block % 2) * PLANES, PLANES), :]
                        for i in range(8)
                    ]
                )
                for i in range(8):
                    dst[pl.ds(f * PLANES * NY + 8 * block + i, PLANES, stride=NY), :] = tiles[i]


def local(states, viscosity, inverse):
    vmem = pl.BlockSpec(memory_space=pltpu.VMEM)
    hbm = pl.BlockSpec(memory_space=pltpu.MemorySpace.HBM)
    f32 = jnp.float32
    sem = pltpu.SemaphoreType.DMA
    back = jax.ShapeDtypeStruct((8, 4, NF, 2, PLANES, NX), f32)
    padded = pltpu.VMEM((NF, 2, NZ + 2 * PAD, NX), f32)
    column = pltpu.VMEM((NF, 2, NZ, NX), f32)
    sems = [
        sem((2,)), sem, sem((3,)), sem((4, 2, 4)), sem((4,)), sem((2,)), sem((2,)), sem((2,)), sem((2,)),
    ]
    packed = 8 * CHUNKS
    res, grad = pl.pallas_call(
        orbit_kernel,
        out_shape=(back, back),
        in_specs=[hbm] * 3,
        out_specs=(vmem, vmem),
        scratch_shapes=[
            pltpu.VMEM((NF * PLANES * NY, NX), f32),
            pltpu.VMEM((PLANES * NY, NX), f32),
            pltpu.VMEM((NF, NZ, NZ), f32),
            pltpu.VMEM((8, 4, NF, 2, PLANES, NX), f32),
            pltpu.VMEM((8, 4, 2, PLANES, NX), f32),
            padded, padded, padded, padded,
            column, column, column, column,
            pltpu.VMEM((4, 8, 2, PLANES, NX), f32),
            pltpu.VMEM((2, NZ, NX), f32),
            pltpu.VMEM((4, 2, NZ, NX), f32),
            pltpu.VMEM((NZ, 2 * NX), f32),
            pltpu.VMEM((NF, NZ, NZ), f32),
            pltpu.VMEM((4, 4, NF, packed, NX), f32),
            pltpu.VMEM((4, 4, NF, packed, NX), f32),
            pltpu.VMEM((4, packed, NX), f32),
            pltpu.VMEM((4, packed, NX), f32),
            sem((4,)), *sems, *sems,
        ],
        compiler_params=pltpu.CompilerParams(
            collective_id=0, has_side_effects=True, vmem_limit_bytes=48 << 20
        ),
        name="orbit",
    )(
        states.reshape(NF * PLANES * NY, NX),
        viscosity.reshape(PLANES * NY, NX),
        inverse,
    )
    flat = jax.ShapeDtypeStruct((NF * PLANES * NY, NX), f32)
    res, grad = pl.pallas_call(
        finish_kernel,
        out_shape=(flat, flat),
        in_specs=[vmem] * 2,
        out_specs=(vmem, vmem),
        compiler_params=pltpu.CompilerParams(vmem_limit_bytes=16 << 20),
        name="finish",
    )(res.reshape(-1, NX), grad.reshape(-1, NX))
    shape = (1, NF, PLANES, NY, NX)
    return res.reshape(shape), grad.reshape(shape)


def solution(mesh):
    spec = P("seg", None, "slab", None, None)
    return jax.shard_map(
        local,
        mesh=mesh,
        in_specs=(spec, P("slab", None, None), P()),
        out_specs=(spec, spec),
        check_vma=False,
    )
```

```python
import jax
import jax.numpy as jnp
from jax import lax
from jax.experimental import pallas as pl
from jax.experimental.pallas import tpu as pltpu
from jax.sharding import PartitionSpec as P

MESH = pl.DeviceIdType.MESH
NZ, NY, NX, NF = 256, 64, 128, 4
SLABS, PLANES = 32, 8
PAD = 8
CHUNK = 64
BLOCKS = CHUNK // 8
CHUNKS = NZ // CHUNK
SIDE = 16
DT = 0.1
GROUPS = ((2, 2), (0, 2))
EAST, WEST, NORTH, SOUTH = range(4)


def patch_of(slab, y_hi):
    return slab // 4, 2 * (((slab // 2) % 2 + y_hi) % 2) + slab % 2


def slab_of(z, quarter, y_hi):
    return z * 4 + ((quarter // 2 + y_hi) % 2) * 2 + quarter % 2


def partner(slab, k):
    z, y, core = slab // 4, (slab // 2) % 2, slab % 2
    j, i = k // 4, k % 4
    dz = 4 + (1 - 2 * (j % 2)) * ((j + 1) // 2)
    return ((z + dz) % 8) * 4 + ((y + 1 - i // 2) % 2) * 2 + (core + 1 - i % 2) % 2


def lane_index(rows):
    return lax.broadcasted_iota(jnp.int32, (rows, NX), 1)


def roll(value, shift):
    shift = shift % NX
    return value if shift == 0 else pltpu.roll(value, shift, 1)


def swap_blocks(groups):
    groups, lane = [list(tiles) for tiles in groups], lane_index(8)
    for bit in (1, 2, 4):
        low = (lane & (SIDE * bit)) == 0
        for i in range(8):
            if not i & bit:
                for tiles in groups:
                    a, b = tiles[i], tiles[i | bit]
                    tiles[i] = jnp.where(low, a, roll(b, SIDE * bit))
                    tiles[i | bit] = jnp.where(low, roll(a, -SIDE * bit), b)
    return groups


def pack_sides(tile_of):
    lane = lane_index(8)
    east = west = north = south = jnp.zeros((8, NX), jnp.float32)
    for b in range(BLOCKS):
        for j in range(2):
            tile, i = tile_of(b, j), 2 * b + j
            here = lane % SIDE == i
            east = jnp.where(here, roll(tile, i), east)
            west = jnp.where(here, roll(tile, i - SIDE + 1), west)
            block = lane // SIDE == b
            if j == 0:
                north = jnp.where(block, roll(tile, SIDE * b), north)
            else:
                south = jnp.where(block, roll(tile, SIDE * b - NX + SIDE), south)
    return east, west, north, south


def neighbours(halves, sides):
    lane = lane_index(CHUNK)
    last, start = lane % SIDE == SIDE - 1, lane % SIDE == 0
    up = [roll(v, -SIDE) for v in halves]
    down = [roll(v, SIDE) for v in halves]

    def spread(side, shift_of):
        return jnp.concatenate([roll(sides[side], shift_of(b)) for b in range(BLOCKS)], axis=0)

    up.append(spread(NORTH, lambda b: NX - SIDE - SIDE * b))
    down.insert(0, spread(SOUTH, lambda b: -SIDE * b))
    found = []
    for j, v in enumerate(halves):
        east = jnp.where(last, spread(EAST, lambda b: SIDE - 1 - 2 * b - j), roll(v, -1))
        west = jnp.where(start, spread(WEST, lambda b: -2 * b - j), roll(v, 1))
        north = jnp.where(lane < NX - SIDE, up[j], up[j + 1])
        south = jnp.where(lane < SIDE, down[j], down[j + 1])
        found.append((east, west, north, south))
    return found


def orbit_kernel(
    states_hbm, visc_hbm, inv_hbm, res_out, grad_out,
    states, visc, inv, send_q, send_v, q, first, adj1, adj2, target, prior, res, grad,
    vset, vcol, faces, work, inv_t, side, halo, vside, vhalo,
    res_in, grad_in, sem_in, recv_q, recv_v, recv_vx, recv_h, recv_vh, recv_t, recv_p, recv_r, recv_g,
    sem_q, sem_v, sem_vx, sem_h, sem_vh, sem_t, sem_p, sem_r, sem_g,
):
    seg, me = lax.axis_index("seg"), lax.axis_index("slab")
    y_hi, x = seg // 4, seg % 4
    z, quarter = patch_of(me, y_hi)
    ahead, behind = (seg + 1) % 8, (seg + 7) % 8
    ahead_slab, behind_slab = slab_of(z, quarter, ahead // 4), slab_of(z, quarter, behind // 4)
    giver = me % 2 + 2 * ((z + (me // 2) % 2) % 2) == x
    takers = (
        (me + SLABS - 4) % SLABS,
        (me + 4) % SLABS,
        slab_of(z, (quarter + 3) % 4, y_hi),
        slab_of(z, (quarter + 1) % 4, y_hi),
    )

    half = NF * PLANES * NY // 2
    loads = (
        pltpu.make_async_copy(visc_hbm, visc, sem_in.at[0]),
        pltpu.make_async_copy(states_hbm.at[pl.ds(half, half)], states.at[pl.ds(half, half)], sem_in.at[1]),
        pltpu.make_async_copy(states_hbm.at[pl.ds(0, half)], states.at[pl.ds(0, half)], sem_in.at[2]),
        pltpu.make_async_copy(inv_hbm, inv, sem_in.at[3]),
    )
    for load in loads:
        load.start()

    barrier = pltpu.get_barrier_semaphore()

    def greet(k, carry):
        pl.semaphore_signal(
            barrier, inc=1, device_id=(seg, partner(me, k)), device_id_type=MESH
        )
        return carry

    lax.fori_loop(0, SLABS - 1, greet, 0)
    pl.semaphore_signal(barrier, inc=1, device_id=(ahead, ahead_slab), device_id_type=MESH)
    pl.semaphore_signal(barrier, inc=1, device_id=(behind, behind_slab), device_id_type=MESH)
    for d in (1, 2, 3):
        pl.semaphore_signal(
            barrier, inc=1, device_id=(y_hi * 4 + (x + d) % 4, me), device_id_type=MESH
        )

    def rows_of(f, y):
        return pl.ds(f * PLANES * NY + y, PLANES, stride=NY)

    def pack(f):
        groups = swap_blocks(
            [[states[rows_of(f, 8 * block + i), :] for i in range(8)] for block in range(NY // 8)]
        )
        for block, tiles in enumerate(groups):
            for i in range(8):
                send_q[i, block // 2, f, block % 2] = tiles[i]

    def unpack(src, dst, f):
        groups = swap_blocks(
            [[src[i, block // 2, f, block % 2] for i in range(8)] for block in range(NY // 8)]
        )
        for block, tiles in enumerate(groups):
            for i in range(8):
                dst[rows_of(f, 8 * block + i), :] = tiles[i]

    own = pl.ds(pl.multiple_of(PLANES * me, PLANES), PLANES)
    own_pad = pl.ds(pl.multiple_of(PLANES * me + PAD, PLANES), PLANES)

    def scatter_states(g, k0, k1):
        f0, n = GROUPS[g]

        def body(k, carry):
            to = partner(me, k)
            zt, qt = patch_of(to, y_hi)
            pltpu.make_async_remote_copy(
                send_q.at[zt, qt, pl.ds(f0, n)], q.at[pl.ds(f0, n), :, own_pad],
                sem_q.at[g], recv_q.at[g], device_id=(seg, to), device_id_type=MESH,
            ).start()
            return carry

        lax.fori_loop(k0, k1, body, 0)

    def wait_many(ref, sem):
        pltpu.make_async_copy(ref, ref, sem).wait()

    loads[0].wait()

    @pl.when(giver)
    def _():
        groups = swap_blocks(
            [[visc[rows_of(0, 8 * block + i), :] for i in range(8)] for block in range(NY // 8)]
        )
        for block, tiles in enumerate(groups):
            for i in range(8):
                send_v[i, block // 2, block % 2] = tiles[i]

    loads[1].wait()
    for f in (2, 3):
        pack(f)
    pl.semaphore_wait(barrier, SLABS + 4)

    @pl.when(giver)
    def _():
        def body(k, carry):
            to = partner(me, k)
            zt, qt = patch_of(to, y_hi)
            pltpu.make_async_remote_copy(
                send_v.at[zt, qt], vset.at[x, z],
                sem_v, recv_v, device_id=(seg, to), device_id_type=MESH,
            ).start()
            return carry

        lax.fori_loop(0, SLABS - 1, body, 0)
        vset[x, z] = send_v[z, quarter]

    scatter_states(0, 0, 10)
    loads[2].wait()
    for f in (0, 1):
        pack(f)
    for f in range(NF):
        q[f, :, own_pad, :] = send_q[z, quarter, f]

    @pl.when(giver)
    def _():
        wait_many(vset.at[x, pl.ds(0, 7)], recv_v)

    @pl.when(jnp.logical_not(giver))
    def _():
        wait_many(vset.at[x, pl.ds(0, 8)], recv_v)

    shares = [
        pltpu.make_async_remote_copy(
            vset.at[x], vset.at[x], sem_vx.at[d - 1], recv_vx.at[d - 1],
            device_id=(y_hi * 4 + (x + d) % 4, me), device_id_type=MESH,
        )
        for d in (1, 2, 3)
    ]
    for share in shares:
        share.start()
    scatter_states(0, 10, SLABS - 1)

    edge = jnp.zeros((NF, 2, PAD, NX), jnp.float32)
    for buf in (q, first, adj1, adj2):
        buf[:, :, 0:PAD, :] = edge
        buf[:, :, PAD + NZ : 2 * PAD + NZ, :] = edge
    loads[3].wait()
    for f in range(NF):
        inv_t[f] = inv[f].T
    for share in shares:
        share.wait_recv()
    for xs in range(4):
        for zs in range(8):
            plane = PLANES * (zs * 4 + ((xs // 2 + zs) % 2) * 2 + xs % 2)
            for j in range(2):
                vcol[j, plane : plane + PLANES, :] = vset[xs, zs, j]

    def over_chunks(body):
        def step(k, carry):
            body(k)
            return carry

        lax.fori_loop(0, CHUNKS, step, 0, unroll=2)

    def at(k, pad=0):
        return pl.ds(pl.multiple_of(k * CHUNK + pad, 8), CHUNK)

    def packed(k):
        return pl.ds(pl.multiple_of(k * 8, 8), 8)

    def visc_copies():
        return [
            pltpu.make_async_remote_copy(
                vside.at[d], vhalo.at[d], sem_vh.at[d], recv_vh.at[d],
                device_id=(seg, takers[d]), device_id_type=MESH,
            )
            for d in range(4)
        ]

    def pack_visc(k):
        sides = pack_sides(lambda b, j: vcol[j, pl.ds(pl.multiple_of(k * CHUNK + 8 * b, 8), 8), :])
        for d in range(4):
            vside[d, packed(k), :] = sides[d]

    over_chunks(pack_visc)
    for copy in visc_copies():
        copy.start()
    scatter_states(1, 0, 8)

    def halo_copies(phase, g):
        f0, n = GROUPS[g]
        fs = pl.ds(f0, n)
        return [
            pltpu.make_async_remote_copy(
                side.at[phase, d, fs], halo.at[phase, d, fs],
                sem_h.at[phase, g, d], recv_h.at[phase, g, d],
                device_id=(seg, takers[d]), device_id_type=MESH,
            )
            for d in range(4)
        ]

    def start_halo(buf, phase, g):
        f0, n = GROUPS[g]

        def body(k):
            for f in range(f0, f0 + n):
                sides = pack_sides(
                    lambda b, j: buf[f, j, pl.ds(pl.multiple_of(k * CHUNK + 8 * b + PAD, 8), 8), :]
                )
                for d in range(4):
                    side[phase, d, f, packed(k), :] = sides[d]

        over_chunks(body)
        for copy in halo_copies(phase, g):
            copy.start()

    def wait_halo(phase, g):
        for copy in halo_copies(phase, g):
            copy.wait_recv()

    def target_copy(g):
        f0, n = GROUPS[g]
        fs = pl.ds(f0, n)
        return pltpu.make_async_remote_copy(
            q.at[fs, :, pl.ds(PAD, NZ)], target.at[fs], sem_t.at[g], recv_t.at[g],
            device_id=(behind, behind_slab), device_id_type=MESH,
        )

    def prior_copy(g):
        f0, n = GROUPS[g]
        fs = pl.ds(f0, n)
        return pltpu.make_async_remote_copy(
            res.at[fs], prior.at[fs], sem_p.at[g], recv_p.at[g],
            device_id=(ahead, ahead_slab), device_id_type=MESH,
        )

    def scatter_back(src, dst, sem, recv, g, k0, k1):
        f0, n = GROUPS[g]
        fs = pl.ds(f0, n)

        def body(k, carry):
            to = partner(me, k)
            pltpu.make_async_remote_copy(
                src.at[fs, :, pl.ds(pl.multiple_of(PLANES * to, PLANES), PLANES)],
                dst.at[z, quarter, fs], sem.at[g], recv.at[g],
                device_id=(seg, to), device_id_type=MESH,
            ).start()
            return carry

        lax.fori_loop(k0, k1, body, 0)

    def return_res(g, k0, k1):
        scatter_back(res, res_in, sem_r, recv_r, g, k0, k1)

    def return_grad(g):
        scatter_back(grad, grad_in, sem_g, recv_g, g, 0, SLABS - 1)

    def keep_own(src, dst, g):
        f0, n = GROUPS[g]
        for f in range(f0, f0 + n):
            dst[z, quarter, f] = src[f, :, own, :]

    def face_values(k):
        halves = [vcol[j, at(k), :] for j in range(2)]
        found = neighbours(halves, [vhalo[d, packed(k), :] for d in range(4)])
        for j in range(2):
            for d in range(4):
                faces[d, j, at(k), :] = 0.5 * (halves[j] + found[j][d])

    def horizontal(buf, phase, f, k, halves):
        found = neighbours(halves, [halo[phase, d, f, packed(k), :] for d in range(4)])
        terms = []
        for j in range(2):
            v, (east, west, north, south) = halves[j], found[j]
            terms.append(
                faces[EAST, j, at(k), :] * (east - v)
                - faces[WEST, j, at(k), :] * (v - west)
                + faces[NORTH, j, at(k), :] * (north - v)
                - faces[SOUTH, j, at(k), :] * (v - south)
            )
        return terms

    def window(buf, f, j, k):
        return buf[f, j, pl.ds(pl.multiple_of(k * CHUNK, 8), CHUNK + 2 * PAD), :]

    def middle(win):
        return win[PAD : PAD + CHUNK]

    def slope(win):
        return win[PAD + 1 : PAD + 1 + CHUNK] - win[PAD - 1 : PAD - 1 + CHUNK]

    def lanes_of(j):
        return slice(j * NX, (j + 1) * NX)

    def fields(g):
        f0, n = GROUPS[g]
        return range(f0, f0 + n)

    def explicit(buf, phase, g):
        def body(k):
            for f in fields(g):
                wins = [window(buf, f, j, k) for j in range(2)]
                halves = [middle(win) for win in wins]
                terms = horizontal(buf, phase, f, k, halves)
                for j in range(2):
                    term = terms[j] - buf[2, j, at(k, PAD), :] * slope(wins[j])
                    if f >= 2:
                        term = term + buf[5 - f, j, at(k, PAD), :]
                    work[f, at(k), lanes_of(j)] = halves[j] + DT * term

        over_chunks(body)

    def adjoint(state, buf, phase, g, minus=None, into=None):
        def body(k):
            for f in fields(g):
                wins = [window(buf, f, j, k) for j in range(2)]
                halves = [middle(win) for win in wins]
                terms = horizontal(buf, phase, f, k, halves)
                for j in range(2):
                    term = terms[j] + slope(window(state, 2, j, k) * wins[j])
                    if f >= 2:
                        term = term + buf[5 - f, j, at(k, PAD), :]
                    if f == 2:
                        total = None
                        for h in range(NF):
                            part = buf[h, j, at(k, PAD), :] * slope(window(state, h, j, k))
                            total = part if total is None else total + part
                        term = term - total
                    out = halves[j] + DT * term
                    if minus is None:
                        work[f, at(k), lanes_of(j)] = out
                    else:
                        into[f, j, at(k), :] = out - minus[f, j, at(k), :]

        over_chunks(body)

    def product(matrix, f):
        return jnp.dot(
            matrix, work[f], precision=lax.Precision.HIGHEST, preferred_element_type=jnp.float32
        )

    def store(buf, f, value):
        for j in range(2):
            buf[f, j, PAD : PAD + NZ, :] = value[:, lanes_of(j)]

    def stage_first(g):
        wait_halo(0, g)
        explicit(q, 0, g)
        for f in fields(g):
            store(first, f, product(inv[f], f))
        start_halo(first, 1, g)

    def stage_residual(g):
        wait_halo(1, g)
        explicit(first, 1, g)
        target_copy(g).wait_recv()
        for f in fields(g):
            end = product(inv[f], f)
            for j in range(2):
                gap = end[:, lanes_of(j)] - target[f, j]
                res[f, j] = gap
                work[f, :, lanes_of(j)] = gap
            store(adj1, f, product(inv_t[f], f))
        start_halo(adj1, 2, g)
        prior_copy(g).start()

    def stage_back(g):
        wait_halo(2, g)
        adjoint(first, adj1, 2, g)
        for f in fields(g):
            store(adj2, f, product(inv_t[f], f))
        start_halo(adj2, 3, g)

    def stage_gradient(g):
        wait_halo(3, g)
        prior_copy(g).wait_recv()
        adjoint(q, adj2, 3, g, minus=prior, into=grad)

    def arrive(g):
        f0, n = GROUPS[g]
        wait_many(q.at[pl.ds(f0, n), :, some], recv_q.at[g])
        start_halo(q, 0, g)
        target_copy(g).start()

    some = pl.ds(0, PLANES * (SLABS - 1))
    last = SLABS - 1
    arrive(0)
    scatter_states(1, 8, 20)
    for copy in visc_copies():
        copy.wait_recv()
    over_chunks(face_values)
    stage_first(0)
    scatter_states(1, 20, last)
    stage_residual(0)
    return_res(0, 0, 6)
    arrive(1)
    return_res(0, 6, 14)
    stage_first(1)
    return_res(0, 14, 23)
    stage_residual(1)
    return_res(0, 23, last)
    stage_back(0)
    return_res(1, 0, 9)
    stage_back(1)
    return_res(1, 9, 18)
    stage_gradient(0)
    return_res(1, 18, last)
    return_grad(0)
    stage_gradient(1)
    return_grad(1)
    for g in range(2):
        keep_own(res, res_in, g)
        keep_own(grad, grad_in, g)

    def collect(recv, src, dst, g):
        f0, n = GROUPS[g]
        wait_many(res.at[pl.ds(f0, n), :, some], recv.at[g])
        for f in fields(g):
            unpack(src, dst, f)

    for g in range(2):
        collect(recv_r, res_in, res_out, g)
    for g in range(2):
        collect(recv_g, grad_in, grad_out, g)

    @pl.when(giver)
    def _():
        wait_many(send_v.at[pl.ds(0, 7)], sem_v)
        wait_many(send_v.at[0, pl.ds(0, 3)], sem_v)

    for copy in shares + visc_copies():
        copy.wait_send()
    for g in range(2):
        fs = pl.ds(GROUPS[g][0], GROUPS[g][1])
        wait_many(q.at[fs, :, some], sem_q.at[g])
        for phase in range(4):
            for copy in halo_copies(phase, g):
                copy.wait_send()
        target_copy(g).wait_send()
        prior_copy(g).wait_send()
        for sem in (sem_r, sem_g):
            wait_many(res.at[fs, :, some], sem.at[g])


def finish_kernel(res_in, grad_in, res_out, grad_out, sem):
    rows = NF * PLANES * NY // 2
    copies = [
        pltpu.make_async_copy(src.at[pl.ds(i * rows, rows)], dst.at[pl.ds(i * rows, rows)], sem.at[n, i])
        for n, (src, dst) in enumerate(((res_in, res_out), (grad_in, grad_out)))
        for i in range(2)
    ]
    for copy in copies:
        copy.start()
    for copy in copies:
        copy.wait()


def local(states, viscosity, inverse):
    vmem = pl.BlockSpec(memory_space=pltpu.VMEM)
    hbm = pl.BlockSpec(memory_space=pltpu.MemorySpace.HBM)
    f32 = jnp.float32
    sem = pltpu.SemaphoreType.DMA
    flat = jax.ShapeDtypeStruct((NF * PLANES * NY, NX), f32)
    spread = pltpu.VMEM((8, 4, NF, 2, PLANES, NX), f32)
    padded = pltpu.VMEM((NF, 2, NZ + 2 * PAD, NX), f32)
    column = pltpu.VMEM((NF, 2, NZ, NX), f32)
    sems = [
        sem((2,)), sem, sem((3,)), sem((4, 2, 4)), sem((4,)), sem((2,)), sem((2,)), sem((2,)), sem((2,)),
    ]
    packed = 8 * CHUNKS
    res, grad = pl.pallas_call(
        orbit_kernel,
        out_shape=(flat, flat),
        in_specs=[hbm] * 3,
        out_specs=(vmem, vmem),
        scratch_shapes=[
            pltpu.VMEM((NF * PLANES * NY, NX), f32),
            pltpu.VMEM((PLANES * NY, NX), f32),
            pltpu.VMEM((NF, NZ, NZ), f32),
            spread,
            pltpu.VMEM((8, 4, 2, PLANES, NX), f32),
            padded, padded, padded, padded,
            column, column, column, column,
            pltpu.VMEM((4, 8, 2, PLANES, NX), f32),
            pltpu.VMEM((2, NZ, NX), f32),
            pltpu.VMEM((4, 2, NZ, NX), f32),
            pltpu.VMEM((NF, NZ, 2 * NX), f32),
            pltpu.VMEM((NF, NZ, NZ), f32),
            pltpu.VMEM((4, 4, NF, packed, NX), f32),
            pltpu.VMEM((4, 4, NF, packed, NX), f32),
            pltpu.VMEM((4, packed, NX), f32),
            pltpu.VMEM((4, packed, NX), f32),
            spread, spread, sem((4,)), *sems, *sems,
        ],
        compiler_params=pltpu.CompilerParams(
            collective_id=0, has_side_effects=True, vmem_limit_bytes=48 << 20
        ),
        name="orbit",
    )(
        *(
            pltpu.with_memory_space_constraint(value, pltpu.MemorySpace.HBM)
            for value in (
                states.reshape(NF * PLANES * NY, NX), viscosity.reshape(PLANES * NY, NX), inverse
            )
        )
    )
    res, grad = pl.pallas_call(
        finish_kernel,
        out_shape=(flat, flat),
        in_specs=[vmem] * 2,
        out_specs=(hbm, hbm),
        scratch_shapes=[sem((2, 2))],
        compiler_params=pltpu.CompilerParams(vmem_limit_bytes=16 << 20),
        name="finish",
    )(res, grad)
    shape = (1, NF, PLANES, NY, NX)
    return res.reshape(shape), grad.reshape(shape)


def solution(mesh):
    spec = P("seg", None, "slab", None, None)
    return jax.shard_map(
        local,
        mesh=mesh,
        in_specs=(spec, P("slab", None, None), P()),
        out_specs=(spec, spec),
        check_vma=False,
    )
```

```python
import jax
import jax.numpy as jnp
from jax import lax
from jax.experimental import pallas as pl
from jax.experimental.pallas import tpu as pltpu
from jax.sharding import PartitionSpec as P

MESH = pl.DeviceIdType.MESH
NZ, NY, NX, NF = 256, 64, 128, 4
SLABS, PLANES = 32, 8
PAD = 8
CHUNK = 64
BLOCKS = CHUNK // 8
CHUNKS = NZ // CHUNK
SIDE = 16
DT = 0.1
GROUPS = ((2, 2), (0, 2))
EAST, WEST, NORTH, SOUTH = range(4)


def patch_of(slab, y_hi):
    return slab // 4, 2 * (((slab // 2) % 2 + y_hi) % 2) + slab % 2


def slab_of(z, quarter, y_hi):
    return z * 4 + ((quarter // 2 + y_hi) % 2) * 2 + quarter % 2


def partner(slab, k):
    z, y, core = slab // 4, (slab // 2) % 2, slab % 2
    j, i = k % 8, k // 8
    dz = 4 + (1 - 2 * (j % 2)) * ((j + 1) // 2)
    return ((z + dz) % 8) * 4 + ((y + 1 - i // 2) % 2) * 2 + (core + 1 - i % 2) % 2


def row_of(tile, i):
    return SIDE * (tile // 2) + tile % 2 + 2 * i


def lane_index(rows):
    return lax.broadcasted_iota(jnp.int32, (rows, NX), 1)


def roll(value, shift):
    shift = shift % NX
    return value if shift == 0 else pltpu.roll(value, shift, 1)


def swap_blocks(groups):
    groups, lane = [list(tiles) for tiles in groups], lane_index(8)
    for bit in (1, 2, 4):
        low = (lane & (SIDE * bit)) == 0
        for i in range(8):
            if not i & bit:
                for tiles in groups:
                    a, b = tiles[i], tiles[i | bit]
                    tiles[i] = jnp.where(low, a, roll(b, SIDE * bit))
                    tiles[i | bit] = jnp.where(low, roll(a, -SIDE * bit), b)
    return groups


def pack_sides(tile_of):
    lane = lane_index(8)
    east = west = north = south = jnp.zeros((8, NX), jnp.float32)
    for b in range(BLOCKS):
        for j in range(2):
            tile, i = tile_of(b, j), 2 * b + j
            moved = roll(tile, i)
            east = jnp.where(lane % SIDE == i, moved, east)
            west = jnp.where(lane % SIDE == (i + SIDE - 1) % SIDE, moved, west)
            if j == 0:
                north = jnp.where(lane // SIDE == b, roll(tile, SIDE * b), north)
            else:
                after = (b + 1) % BLOCKS
                south = jnp.where(lane // SIDE == after, roll(tile, SIDE * (b + 2)), south)
    return east, west, north, south


def neighbours(halves, sides):
    lane, few = lane_index(CHUNK), lane_index(8)
    last, start = lane % SIDE == SIDE - 1, lane % SIDE == 0
    even_lane, even_block = few % 2 == 0, (few // SIDE) % 2 == 0
    east, west, north, south = sides
    west = roll(west, -2 * (SIDE - 1))
    along_x = (jnp.where(even_lane, east, west), jnp.where(even_lane, west, east))
    along_y = (jnp.where(even_block, north, south), jnp.where(even_block, south, north))
    edge_y = jnp.concatenate(
        [roll(along_y[b % 2], NX - SIDE - SIDE * b) for b in range(BLOCKS)], axis=0
    )
    norths = (halves[1], jnp.where(lane < NX - SIDE, roll(halves[0], -SIDE), edge_y))
    souths = (jnp.where(lane < SIDE, edge_y, roll(halves[1], SIDE)), halves[0])
    found = []
    for j, v in enumerate(halves):
        edge_x = jnp.concatenate(
            [roll(along_x[j], SIDE - 1 - 2 * b - j) for b in range(BLOCKS)], axis=0
        )
        found.append(
            (
                jnp.where(last, edge_x, roll(v, -1)),
                jnp.where(start, edge_x, roll(v, 1)),
                norths[j],
                souths[j],
            )
        )
    return found


def orbit_kernel(
    states_hbm, visc_hbm, inv_hbm, res_out, grad_out,
    states, visc, inv, send_q, send_v, q, first, adj1, adj2, target, prior, res, grad,
    vset, vcol, faces, work, inv_t, side, halo, vside, vhalo,
    res_in, grad_in, sem_in, recv_q, recv_v, recv_vx, recv_h, recv_vh, recv_t, recv_p, recv_r, recv_g,
    sem_q, sem_v, sem_vx, sem_h, sem_vh, sem_t, sem_p, sem_r, sem_g,
):
    seg, me = lax.axis_index("seg"), lax.axis_index("slab")
    y_hi, x = seg // 4, seg % 4
    z, quarter = patch_of(me, y_hi)
    ahead, behind = (seg + 1) % 8, (seg + 7) % 8
    ahead_slab, behind_slab = slab_of(z, quarter, ahead // 4), slab_of(z, quarter, behind // 4)
    giver = me % 2 + 2 * ((z + (me // 2) % 2) % 2) == x
    takers = (
        (me + SLABS - 4) % SLABS,
        (me + 4) % SLABS,
        slab_of(z, (quarter + 3) % 4, y_hi),
        slab_of(z, (quarter + 1) % 4, y_hi),
    )

    half = NF * PLANES * NY // 2
    loads = (
        pltpu.make_async_copy(states_hbm.at[pl.ds(half, half)], states.at[pl.ds(half, half)], sem_in.at[0]),
        pltpu.make_async_copy(visc_hbm, visc, sem_in.at[1]),
        pltpu.make_async_copy(states_hbm.at[pl.ds(0, half)], states.at[pl.ds(0, half)], sem_in.at[2]),
        pltpu.make_async_copy(inv_hbm, inv, sem_in.at[3]),
    )
    for load in loads:
        load.start()

    barrier = pltpu.get_barrier_semaphore()

    def greet(k, carry):
        pl.semaphore_signal(
            barrier, inc=1, device_id=(seg, partner(me, k)), device_id_type=MESH
        )
        return carry

    lax.fori_loop(0, SLABS - 1, greet, 0)
    pl.semaphore_signal(barrier, inc=1, device_id=(ahead, ahead_slab), device_id_type=MESH)
    pl.semaphore_signal(barrier, inc=1, device_id=(behind, behind_slab), device_id_type=MESH)
    for d in (1, 2, 3):
        pl.semaphore_signal(
            barrier, inc=1, device_id=(y_hi * 4 + (x + d) % 4, me), device_id_type=MESH
        )

    def rows_of(f, y):
        return pl.ds(f * PLANES * NY + y, PLANES, stride=NY)

    def pack(f):
        groups = swap_blocks(
            [[states[rows_of(f, row_of(block, i)), :] for i in range(8)] for block in range(NY // 8)]
        )
        for block, tiles in enumerate(groups):
            for i in range(8):
                send_q[i, block // 2, f, block % 2] = tiles[i]

    def unpack(src, dst, f):
        groups = swap_blocks(
            [[src[i, block // 2, f, block % 2] for i in range(8)] for block in range(NY // 8)]
        )
        for block, tiles in enumerate(groups):
            for i in range(8):
                dst[rows_of(f, row_of(block, i)), :] = tiles[i]

    own = pl.ds(pl.multiple_of(PLANES * me, PLANES), PLANES)
    own_pad = pl.ds(pl.multiple_of(PLANES * me + PAD, PLANES), PLANES)

    def scatter_states(g, k0, k1):
        f0, n = GROUPS[g]

        def body(k, carry):
            to = partner(me, k)
            zt, qt = patch_of(to, y_hi)
            pltpu.make_async_remote_copy(
                send_q.at[zt, qt, pl.ds(f0, n)], q.at[pl.ds(f0, n), :, own_pad],
                sem_q.at[g], recv_q.at[g, k % 8], device_id=(seg, to), device_id_type=MESH,
            ).start()
            return carry

        lax.fori_loop(k0, k1, body, 0)

    def wait_many(ref, sem):
        pltpu.make_async_copy(ref, ref, sem).wait()

    loads[0].wait()
    for f in (2, 3):
        pack(f)
    pl.semaphore_wait(barrier, SLABS + 4)
    scatter_states(0, 0, 16)
    loads[1].wait()

    @pl.when(giver)
    def _():
        groups = swap_blocks(
            [[visc[rows_of(0, row_of(block, i)), :] for i in range(8)] for block in range(NY // 8)]
        )
        for block, tiles in enumerate(groups):
            for i in range(8):
                send_v[i, block // 2, block % 2] = tiles[i]

        def body(k, carry):
            to = partner(me, k)
            zt, qt = patch_of(to, y_hi)
            pltpu.make_async_remote_copy(
                send_v.at[zt, qt], vset.at[x, z],
                sem_v, recv_v, device_id=(seg, to), device_id_type=MESH,
            ).start()
            return carry

        lax.fori_loop(0, SLABS - 1, body, 0)
        vset[x, z] = send_v[z, quarter]

    scatter_states(0, 16, SLABS - 1)
    loads[2].wait()
    for f in (0, 1):
        pack(f)
    for f in range(NF):
        q[f, :, own_pad, :] = send_q[z, quarter, f]
    scatter_states(1, 0, 10)

    @pl.when(giver)
    def _():
        wait_many(vset.at[x, pl.ds(0, 7)], recv_v)

    @pl.when(jnp.logical_not(giver))
    def _():
        wait_many(vset.at[x, pl.ds(0, 8)], recv_v)

    shares = [
        pltpu.make_async_remote_copy(
            vset.at[x], vset.at[x], sem_vx.at[d - 1], recv_vx.at[d - 1],
            device_id=(y_hi * 4 + (x + d) % 4, me), device_id_type=MESH,
        )
        for d in (1, 2, 3)
    ]
    for share in shares:
        share.start()

    edge = jnp.zeros((NF, 2, PAD, NX), jnp.float32)
    for buf in (q, first, adj1, adj2):
        buf[:, :, 0:PAD, :] = edge
        buf[:, :, PAD + NZ : 2 * PAD + NZ, :] = edge
    loads[3].wait()
    for f in range(NF):
        inv_t[f] = inv[f].T

    def over_chunks(body):
        def step(k, carry):
            body(k)
            return carry

        lax.fori_loop(0, CHUNKS, step, 0, unroll=2)

    def at(k, pad=0):
        return pl.ds(pl.multiple_of(k * CHUNK + pad, 8), CHUNK)

    def packed(k):
        return pl.ds(pl.multiple_of(k * 8, 8), 8)

    def visc_copies():
        return [
            pltpu.make_async_remote_copy(
                vside.at[d], vhalo.at[d], sem_vh.at[d], recv_vh.at[d],
                device_id=(seg, takers[d]), device_id_type=MESH,
            )
            for d in range(4)
        ]

    def pack_visc(k):
        sides = pack_sides(lambda b, j: vcol[j, pl.ds(pl.multiple_of(k * CHUNK + 8 * b, 8), 8), :])
        for d in range(4):
            vside[d, packed(k), :] = sides[d]


    def halo_copies(phase, g):
        f0, n = GROUPS[g]
        fs = pl.ds(f0, n)
        return [
            pltpu.make_async_remote_copy(
                side.at[phase, d, fs], halo.at[phase, d, fs],
                sem_h.at[phase, g, d], recv_h.at[phase, g, d],
                device_id=(seg, takers[d]), device_id_type=MESH,
            )
            for d in range(4)
        ]

    def start_halo(buf, phase, g):
        f0, n = GROUPS[g]

        def body(k):
            for f in range(f0, f0 + n):
                sides = pack_sides(
                    lambda b, j: buf[f, j, pl.ds(pl.multiple_of(k * CHUNK + 8 * b + PAD, 8), 8), :]
                )
                for d in range(4):
                    side[phase, d, f, packed(k), :] = sides[d]

        over_chunks(body)
        for copy in halo_copies(phase, g):
            copy.start()

    def wait_halo(phase, g):
        for copy in halo_copies(phase, g):
            copy.wait_recv()

    def forward_target(g):
        f0, n = GROUPS[g]
        fs = pl.ds(f0, n)
        span = 4 * PLANES
        for j in range(8):
            dz = 4 + (1 - 2 * (j % 2)) * ((j + 1) // 2)
            count = span if dz else span - PLANES
            wait_many(q.at[fs, :, pl.ds(0, count)], recv_q.at[g, j])
            z0 = pl.multiple_of(((z + 8 - dz) % 8) * span, span)
            pltpu.make_async_remote_copy(
                q.at[fs, :, pl.ds(PAD + z0, span)], target.at[fs, :, pl.ds(z0, span)],
                sem_t.at[g], recv_t.at[g],
                device_id=(behind, behind_slab), device_id_type=MESH,
            ).start()

    def wait_target(g, sem):
        f0, n = GROUPS[g]
        wait_many(target.at[pl.ds(f0, n)], sem.at[g])

    def prior_copy(g):
        f0, n = GROUPS[g]
        fs = pl.ds(f0, n)
        return pltpu.make_async_remote_copy(
            res.at[fs], prior.at[fs], sem_p.at[g], recv_p.at[g],
            device_id=(ahead, ahead_slab), device_id_type=MESH,
        )

    def scatter_back(src, dst, sem, recv, g, k0, k1):
        f0, n = GROUPS[g]
        fs = pl.ds(f0, n)

        def body(k, carry):
            to = partner(me, k)
            pltpu.make_async_remote_copy(
                src.at[fs, :, pl.ds(pl.multiple_of(PLANES * to, PLANES), PLANES)],
                dst.at[z, quarter, fs], sem.at[g], recv.at[g],
                device_id=(seg, to), device_id_type=MESH,
            ).start()
            return carry

        lax.fori_loop(k0, k1, body, 0)

    def return_res(g, k0, k1):
        scatter_back(res, res_in, sem_r, recv_r, g, k0, k1)

    def return_grad(g):
        scatter_back(grad, grad_in, sem_g, recv_g, g, 0, SLABS - 1)

    def keep_own(src, dst, g):
        f0, n = GROUPS[g]
        for f in range(f0, f0 + n):
            dst[z, quarter, f] = src[f, :, own, :]

    def face_values(k):
        halves = [vcol[j, at(k), :] for j in range(2)]
        found = neighbours(halves, [vhalo[d, packed(k), :] for d in range(4)])
        for j in range(2):
            for d in range(4):
                faces[d, j, at(k), :] = 0.5 * (halves[j] + found[j][d])

    def horizontal(buf, phase, f, k, halves):
        found = neighbours(halves, [halo[phase, d, f, packed(k), :] for d in range(4)])
        terms = []
        for j in range(2):
            v, (east, west, north, south) = halves[j], found[j]
            terms.append(
                faces[EAST, j, at(k), :] * (east - v)
                - faces[WEST, j, at(k), :] * (v - west)
                + faces[NORTH, j, at(k), :] * (north - v)
                - faces[SOUTH, j, at(k), :] * (v - south)
            )
        return terms

    def window(buf, f, j, k):
        return buf[f, j, pl.ds(pl.multiple_of(k * CHUNK, 8), CHUNK + 2 * PAD), :]

    def middle(win):
        return win[PAD : PAD + CHUNK]

    def slope(win):
        return win[PAD + 1 : PAD + 1 + CHUNK] - win[PAD - 1 : PAD - 1 + CHUNK]

    def lanes_of(j):
        return slice(j * NX, (j + 1) * NX)

    def fields(g):
        f0, n = GROUPS[g]
        return range(f0, f0 + n)

    def explicit(buf, phase, g):
        def body(k):
            for f in fields(g):
                wins = [window(buf, f, j, k) for j in range(2)]
                halves = [middle(win) for win in wins]
                terms = horizontal(buf, phase, f, k, halves)
                for j in range(2):
                    term = terms[j] - buf[2, j, at(k, PAD), :] * slope(wins[j])
                    if f >= 2:
                        term = term + buf[5 - f, j, at(k, PAD), :]
                    work[f, at(k), lanes_of(j)] = halves[j] + DT * term

        over_chunks(body)

    def adjoint(state, buf, phase, g, minus=None, into=None):
        def body(k):
            for f in fields(g):
                wins = [window(buf, f, j, k) for j in range(2)]
                halves = [middle(win) for win in wins]
                terms = horizontal(buf, phase, f, k, halves)
                for j in range(2):
                    term = terms[j] + slope(window(state, 2, j, k) * wins[j])
                    if f >= 2:
                        term = term + buf[5 - f, j, at(k, PAD), :]
                    if f == 2:
                        total = None
                        for h in range(NF):
                            part = buf[h, j, at(k, PAD), :] * slope(window(state, h, j, k))
                            total = part if total is None else total + part
                        term = term - total
                    out = halves[j] + DT * term
                    if minus is None:
                        work[f, at(k), lanes_of(j)] = out
                    else:
                        into[f, j, at(k), :] = out - minus[f, j, at(k), :]

        over_chunks(body)

    def product(matrix, f):
        return jnp.dot(
            matrix, work[f], precision=lax.Precision.HIGHEST, preferred_element_type=jnp.float32
        )

    def store(buf, f, value):
        for j in range(2):
            buf[f, j, PAD : PAD + NZ, :] = value[:, lanes_of(j)]

    def stage_first(g):
        wait_halo(0, g)
        explicit(q, 0, g)
        for f in fields(g):
            store(first, f, product(inv[f], f))
        start_halo(first, 1, g)

    def stage_residual(g):
        wait_halo(1, g)
        explicit(first, 1, g)
        wait_target(g, recv_t)
        for f in fields(g):
            end = product(inv[f], f)
            for j in range(2):
                gap = end[:, lanes_of(j)] - target[f, j]
                res[f, j] = gap
                work[f, :, lanes_of(j)] = gap
            store(adj1, f, product(inv_t[f], f))
        start_halo(adj1, 2, g)
        prior_copy(g).start()

    def stage_back(g):
        wait_halo(2, g)
        adjoint(first, adj1, 2, g)
        for f in fields(g):
            store(adj2, f, product(inv_t[f], f))
        start_halo(adj2, 3, g)

    def stage_gradient(g):
        wait_halo(3, g)
        prior_copy(g).wait_recv()
        adjoint(q, adj2, 3, g, minus=prior, into=grad)

    some = pl.ds(0, PLANES * (SLABS - 1))
    last = SLABS - 1
    forward_target(0)
    start_halo(q, 0, 0)
    scatter_states(1, 10, 16)
    for share in shares:
        share.wait_recv()
    for xs in range(4):
        for zs in range(8):
            plane = PLANES * (zs * 4 + ((xs // 2 + zs) % 2) * 2 + xs % 2)
            for j in range(2):
                vcol[j, plane : plane + PLANES, :] = vset[xs, zs, j]
    over_chunks(pack_visc)
    for copy in visc_copies():
        copy.start()
    scatter_states(1, 16, 27)
    for copy in visc_copies():
        copy.wait_recv()
    over_chunks(face_values)
    stage_first(0)
    scatter_states(1, 27, last)
    stage_residual(0)
    return_res(0, 0, 8)
    forward_target(1)
    start_halo(q, 0, 1)
    return_res(0, 8, 20)
    stage_first(1)
    return_res(0, 20, last)
    stage_residual(1)
    return_res(1, 0, 10)
    stage_back(0)
    return_res(1, 10, 20)
    stage_back(1)
    return_res(1, 20, last)
    stage_gradient(0)
    return_grad(0)
    stage_gradient(1)
    return_grad(1)
    for g in range(2):
        keep_own(res, res_in, g)
        keep_own(grad, grad_in, g)

    def collect(recv, src, dst, g):
        f0, n = GROUPS[g]
        wait_many(res.at[pl.ds(f0, n), :, some], recv.at[g])
        for f in fields(g):
            unpack(src, dst, f)

    for g in range(2):
        collect(recv_r, res_in, res_out, g)
    for g in range(2):
        collect(recv_g, grad_in, grad_out, g)

    @pl.when(giver)
    def _():
        wait_many(send_v.at[pl.ds(0, 7)], sem_v)
        wait_many(send_v.at[0, pl.ds(0, 3)], sem_v)

    for copy in shares + visc_copies():
        copy.wait_send()
    for g in range(2):
        fs = pl.ds(GROUPS[g][0], GROUPS[g][1])
        wait_many(q.at[fs, :, some], sem_q.at[g])
        for phase in range(4):
            for copy in halo_copies(phase, g):
                copy.wait_send()
        wait_target(g, sem_t)
        prior_copy(g).wait_send()
        for sem in (sem_r, sem_g):
            wait_many(res.at[fs, :, some], sem.at[g])


def finish_kernel(res_in, grad_in, res_out, grad_out, sem):
    rows = NF * PLANES * NY // 2
    copies = [
        pltpu.make_async_copy(src.at[pl.ds(i * rows, rows)], dst.at[pl.ds(i * rows, rows)], sem.at[n, i])
        for n, (src, dst) in enumerate(((res_in, res_out), (grad_in, grad_out)))
        for i in range(2)
    ]
    for copy in copies:
        copy.start()
    for copy in copies:
        copy.wait()


def local(states, viscosity, inverse):
    vmem = pl.BlockSpec(memory_space=pltpu.VMEM)
    hbm = pl.BlockSpec(memory_space=pltpu.MemorySpace.HBM)
    f32 = jnp.float32
    sem = pltpu.SemaphoreType.DMA
    flat = jax.ShapeDtypeStruct((NF * PLANES * NY, NX), f32)
    spread = pltpu.VMEM((8, 4, NF, 2, PLANES, NX), f32)
    padded = pltpu.VMEM((NF, 2, NZ + 2 * PAD, NX), f32)
    column = pltpu.VMEM((NF, 2, NZ, NX), f32)
    sems = [sem((3,)), sem((4, 2, 4)), sem((4,)), sem((2,)), sem((2,)), sem((2,)), sem((2,))]
    packed = 8 * CHUNKS
    res, grad = pl.pallas_call(
        orbit_kernel,
        out_shape=(flat, flat),
        in_specs=[hbm] * 3,
        out_specs=(vmem, vmem),
        scratch_shapes=[
            pltpu.VMEM((NF * PLANES * NY, NX), f32),
            pltpu.VMEM((PLANES * NY, NX), f32),
            pltpu.VMEM((NF, NZ, NZ), f32),
            spread,
            pltpu.VMEM((8, 4, 2, PLANES, NX), f32),
            padded, padded, padded, padded,
            column, column, column, column,
            pltpu.VMEM((4, 8, 2, PLANES, NX), f32),
            pltpu.VMEM((2, NZ, NX), f32),
            pltpu.VMEM((4, 2, NZ, NX), f32),
            pltpu.VMEM((NF, NZ, 2 * NX), f32),
            pltpu.VMEM((NF, NZ, NZ), f32),
            pltpu.VMEM((4, 4, NF, packed, NX), f32),
            pltpu.VMEM((4, 4, NF, packed, NX), f32),
            pltpu.VMEM((4, packed, NX), f32),
            pltpu.VMEM((4, packed, NX), f32),
            spread, spread, sem((4,)), sem((2, 8)), sem, *sems, sem((2,)), sem, *sems,
        ],
        compiler_params=pltpu.CompilerParams(
            collective_id=0, has_side_effects=True, vmem_limit_bytes=48 << 20
        ),
        name="orbit",
    )(
        *(
            pltpu.with_memory_space_constraint(value, pltpu.MemorySpace.HBM)
            for value in (
                states.reshape(NF * PLANES * NY, NX), viscosity.reshape(PLANES * NY, NX), inverse
            )
        )
    )
    res, grad = pl.pallas_call(
        finish_kernel,
        out_shape=(flat, flat),
        in_specs=[vmem] * 2,
        out_specs=(hbm, hbm),
        scratch_shapes=[sem((2, 2))],
        compiler_params=pltpu.CompilerParams(vmem_limit_bytes=16 << 20),
        name="finish",
    )(res, grad)
    shape = (1, NF, PLANES, NY, NX)
    return res.reshape(shape), grad.reshape(shape)


def solution(mesh):
    spec = P("seg", None, "slab", None, None)
    return jax.shard_map(
        local,
        mesh=mesh,
        in_specs=(spec, P("slab", None, None), P()),
        out_specs=(spec, spec),
        check_vma=False,
    )
```

```python
import jax
import jax.numpy as jnp
from jax import lax
from jax.experimental import pallas as pl
from jax.experimental.pallas import tpu as pltpu
from jax.sharding import PartitionSpec as P

MESH = pl.DeviceIdType.MESH
NZ, NY, NX, NF = 256, 64, 128, 4
SLABS, PLANES = 32, 8
PAD = 8
CHUNK = 64
BLOCKS = CHUNK // 8
CHUNKS = NZ // CHUNK
SIDE = 16
DT = 0.1
GROUPS = ((2, 2), (0, 2))
EAST, WEST, NORTH, SOUTH = range(4)


def patch_of(slab, y_hi):
    return slab // 4, 2 * (((slab // 2) % 2 + y_hi) % 2) + slab % 2


def slab_of(z, quarter, y_hi):
    return z * 4 + ((quarter // 2 + y_hi) % 2) * 2 + quarter % 2


def partner(slab, k):
    z, y, core = slab // 4, (slab // 2) % 2, slab % 2
    j, i = k % 8, k // 8
    dz = 4 + (1 - 2 * (j % 2)) * ((j + 1) // 2)
    return ((z + dz) % 8) * 4 + ((y + 1 - i // 2) % 2) * 2 + (core + 1 - i % 2) % 2


def row_of(tile, i):
    return SIDE * (tile // 2) + tile % 2 + 2 * i


def lane_index(rows):
    return lax.broadcasted_iota(jnp.int32, (rows, NX), 1)


def roll(value, shift):
    shift = shift % NX
    return value if shift == 0 else pltpu.roll(value, shift, 1)


def swap_blocks(groups):
    groups, lane = [list(tiles) for tiles in groups], lane_index(8)
    for bit in (1, 2, 4):
        low = (lane & (SIDE * bit)) == 0
        for i in range(8):
            if not i & bit:
                for tiles in groups:
                    a, b = tiles[i], tiles[i | bit]
                    tiles[i] = jnp.where(low, a, roll(b, SIDE * bit))
                    tiles[i | bit] = jnp.where(low, roll(a, -SIDE * bit), b)
    return groups


def pack_sides(tile_of):
    lane = lane_index(8)
    east = west = north = south = jnp.zeros((8, NX), jnp.float32)
    for b in range(BLOCKS):
        for j in range(2):
            tile, i = tile_of(b, j), 2 * b + j
            moved = roll(tile, i)
            east = jnp.where(lane % SIDE == i, moved, east)
            west = jnp.where(lane % SIDE == (i + SIDE - 1) % SIDE, moved, west)
            if j == 0:
                north = jnp.where(lane // SIDE == b, roll(tile, SIDE * b), north)
            else:
                after = (b + 1) % BLOCKS
                south = jnp.where(lane // SIDE == after, roll(tile, SIDE * (b + 2)), south)
    return east, west, north, south


def neighbours(halves, sides):
    lane, few = lane_index(CHUNK), lane_index(8)
    last, start = lane % SIDE == SIDE - 1, lane % SIDE == 0
    even_lane, even_block = few % 2 == 0, (few // SIDE) % 2 == 0
    east, west, north, south = sides
    west = roll(west, -2 * (SIDE - 1))
    along_x = (jnp.where(even_lane, east, west), jnp.where(even_lane, west, east))
    along_y = (jnp.where(even_block, north, south), jnp.where(even_block, south, north))
    edge_y = jnp.concatenate(
        [roll(along_y[b % 2], NX - SIDE - SIDE * b) for b in range(BLOCKS)], axis=0
    )
    norths = (halves[1], jnp.where(lane < NX - SIDE, roll(halves[0], -SIDE), edge_y))
    souths = (jnp.where(lane < SIDE, edge_y, roll(halves[1], SIDE)), halves[0])
    found = []
    for j, v in enumerate(halves):
        edge_x = jnp.concatenate(
            [roll(along_x[j], SIDE - 1 - 2 * b - j) for b in range(BLOCKS)], axis=0
        )
        found.append(
            (
                jnp.where(last, edge_x, roll(v, -1)),
                jnp.where(start, edge_x, roll(v, 1)),
                norths[j],
                souths[j],
            )
        )
    return found


def orbit_kernel(
    states_hbm, visc_hbm, inv_hbm, res_out, grad_out,
    states, visc, inv, send_q, send_v, q, first, adj1, adj2, target, prior, res, grad,
    vset, vcol, faces, work, inv_t, side, halo, vside, vhalo,
    res_in, grad_in, sem_in, recv_q, recv_v, recv_vx, recv_h, recv_vh, recv_t, recv_p, recv_r, recv_g,
    sem_q, sem_v, sem_vx, sem_h, sem_vh, sem_t, sem_p, sem_r, sem_g,
):
    seg, me = lax.axis_index("seg"), lax.axis_index("slab")
    y_hi, x = seg // 4, seg % 4
    z, quarter = patch_of(me, y_hi)
    ahead, behind = (seg + 1) % 8, (seg + 7) % 8
    ahead_slab, behind_slab = slab_of(z, quarter, ahead // 4), slab_of(z, quarter, behind // 4)
    giver = me % 2 + 2 * ((z + (me // 2) % 2) % 2) == x
    takers = (
        (me + SLABS - 4) % SLABS,
        (me + 4) % SLABS,
        slab_of(z, (quarter + 3) % 4, y_hi),
        slab_of(z, (quarter + 1) % 4, y_hi),
    )

    half = NF * PLANES * NY // 2
    loads = (
        pltpu.make_async_copy(states_hbm.at[pl.ds(half, half)], states.at[pl.ds(half, half)], sem_in.at[0]),
        pltpu.make_async_copy(visc_hbm, visc, sem_in.at[1]),
        pltpu.make_async_copy(states_hbm.at[pl.ds(0, half)], states.at[pl.ds(0, half)], sem_in.at[2]),
        pltpu.make_async_copy(inv_hbm, inv, sem_in.at[3]),
    )
    for load in loads:
        load.start()

    barrier = pltpu.get_barrier_semaphore()

    def greet(k, carry):
        pl.semaphore_signal(
            barrier, inc=1, device_id=(seg, partner(me, k)), device_id_type=MESH
        )
        return carry

    lax.fori_loop(0, SLABS - 1, greet, 0)
    pl.semaphore_signal(barrier, inc=1, device_id=(ahead, ahead_slab), device_id_type=MESH)
    pl.semaphore_signal(barrier, inc=1, device_id=(behind, behind_slab), device_id_type=MESH)
    for d in (1, 2, 3):
        pl.semaphore_signal(
            barrier, inc=1, device_id=(y_hi * 4 + (x + d) % 4, me), device_id_type=MESH
        )

    def rows_of(f, y):
        return pl.ds(f * PLANES * NY + y, PLANES, stride=NY)

    def pack(f):
        groups = swap_blocks(
            [[states[rows_of(f, row_of(block, i)), :] for i in range(8)] for block in range(NY // 8)]
        )
        for block, tiles in enumerate(groups):
            for i in range(8):
                send_q[i, block // 2, f, block % 2] = tiles[i]

    def unpack(src, dst, f):
        groups = swap_blocks(
            [[src[i, block // 2, f, block % 2] for i in range(8)] for block in range(NY // 8)]
        )
        for block, tiles in enumerate(groups):
            for i in range(8):
                dst[rows_of(f, row_of(block, i)), :] = tiles[i]

    own = pl.ds(pl.multiple_of(PLANES * me, PLANES), PLANES)
    own_pad = pl.ds(pl.multiple_of(PLANES * me + PAD, PLANES), PLANES)

    def scatter_states(g, k0, k1):
        f0, n = GROUPS[g]

        def body(k, carry):
            to = partner(me, k)
            zt, qt = patch_of(to, y_hi)
            pltpu.make_async_remote_copy(
                send_q.at[zt, qt, pl.ds(f0, n)], q.at[pl.ds(f0, n), :, own_pad],
                sem_q.at[g], recv_q.at[g, k % 8], device_id=(seg, to), device_id_type=MESH,
            ).start()
            return carry

        lax.fori_loop(k0, k1, body, 0)

    def wait_many(ref, sem):
        pltpu.make_async_copy(ref, ref, sem).wait()

    loads[0].wait()
    for f in (2, 3):
        pack(f)
    pl.semaphore_wait(barrier, SLABS + 4)
    scatter_states(0, 0, 16)
    loads[1].wait()

    @pl.when(giver)
    def _():
        groups = swap_blocks(
            [[visc[rows_of(0, row_of(block, i)), :] for i in range(8)] for block in range(NY // 8)]
        )
        for block, tiles in enumerate(groups):
            for i in range(8):
                send_v[i, block // 2, block % 2] = tiles[i]

        def body(k, carry):
            to = partner(me, k)
            zt, qt = patch_of(to, y_hi)
            pltpu.make_async_remote_copy(
                send_v.at[zt, qt], vset.at[x, z],
                sem_v, recv_v, device_id=(seg, to), device_id_type=MESH,
            ).start()
            return carry

        lax.fori_loop(0, SLABS - 1, body, 0)
        vset[x, z] = send_v[z, quarter]

    scatter_states(0, 16, SLABS - 1)
    loads[2].wait()
    for f in (0, 1):
        pack(f)
    for f in range(NF):
        q[f, :, own_pad, :] = send_q[z, quarter, f]

    @pl.when(giver)
    def _():
        wait_many(vset.at[x, pl.ds(0, 7)], recv_v)

    @pl.when(jnp.logical_not(giver))
    def _():
        wait_many(vset.at[x, pl.ds(0, 8)], recv_v)

    shares = [
        pltpu.make_async_remote_copy(
            vset.at[x], vset.at[x], sem_vx.at[d - 1], recv_vx.at[d - 1],
            device_id=(y_hi * 4 + (x + d) % 4, me), device_id_type=MESH,
        )
        for d in (1, 2, 3)
    ]
    for share in shares:
        share.start()
    scatter_states(1, 0, 10)

    edge = jnp.zeros((NF, 2, PAD, NX), jnp.float32)
    for buf in (q, first, adj1, adj2):
        buf[:, :, 0:PAD, :] = edge
        buf[:, :, PAD + NZ : 2 * PAD + NZ, :] = edge
    loads[3].wait()
    for f in range(NF):
        inv_t[f] = inv[f].T

    def over_chunks(body):
        def step(k, carry):
            body(k)
            return carry

        lax.fori_loop(0, CHUNKS, step, 0, unroll=2)

    def at(k, pad=0):
        return pl.ds(pl.multiple_of(k * CHUNK + pad, 8), CHUNK)

    def packed(k):
        return pl.ds(pl.multiple_of(k * 8, 8), 8)

    def visc_copies():
        return [
            pltpu.make_async_remote_copy(
                vside.at[d], vhalo.at[d], sem_vh.at[d], recv_vh.at[d],
                device_id=(seg, takers[d]), device_id_type=MESH,
            )
            for d in range(4)
        ]

    def pack_visc(k):
        sides = pack_sides(lambda b, j: vcol[j, pl.ds(pl.multiple_of(k * CHUNK + 8 * b, 8), 8), :])
        for d in range(4):
            vside[d, packed(k), :] = sides[d]


    def halo_copies(phase, g):
        f0, n = GROUPS[g]
        fs = pl.ds(f0, n)
        return [
            pltpu.make_async_remote_copy(
                side.at[phase, d, fs], halo.at[phase, d, fs],
                sem_h.at[phase, g, d], recv_h.at[phase, g, d],
                device_id=(seg, takers[d]), device_id_type=MESH,
            )
            for d in range(4)
        ]

    def start_halo(buf, phase, g):
        f0, n = GROUPS[g]

        def body(k):
            for f in range(f0, f0 + n):
                sides = pack_sides(
                    lambda b, j: buf[f, j, pl.ds(pl.multiple_of(k * CHUNK + 8 * b + PAD, 8), 8), :]
                )
                for d in range(4):
                    side[phase, d, f, packed(k), :] = sides[d]

        over_chunks(body)
        for copy in halo_copies(phase, g):
            copy.start()

    def wait_halo(phase, g):
        for copy in halo_copies(phase, g):
            copy.wait_recv()

    def forward_target(g):
        f0, n = GROUPS[g]
        fs = pl.ds(f0, n)
        span = 4 * PLANES
        for j in range(8):
            dz = 4 + (1 - 2 * (j % 2)) * ((j + 1) // 2)
            count = span if dz else span - PLANES
            wait_many(q.at[fs, :, pl.ds(0, count)], recv_q.at[g, j])
            z0 = pl.multiple_of(((z + 8 - dz) % 8) * span, span)
            pltpu.make_async_remote_copy(
                q.at[fs, :, pl.ds(PAD + z0, span)], target.at[fs, :, pl.ds(z0, span)],
                sem_t.at[g], recv_t.at[g],
                device_id=(behind, behind_slab), device_id_type=MESH,
            ).start()

    def wait_target(g, sem):
        f0, n = GROUPS[g]
        wait_many(target.at[pl.ds(f0, n)], sem.at[g])

    def prior_copy(g):
        f0, n = GROUPS[g]
        fs = pl.ds(f0, n)
        return pltpu.make_async_remote_copy(
            res.at[fs], prior.at[fs], sem_p.at[g], recv_p.at[g],
            device_id=(ahead, ahead_slab), device_id_type=MESH,
        )

    def scatter_back(src, dst, sem, recv, g, k0, k1):
        f0, n = GROUPS[g]
        fs = pl.ds(f0, n)

        def body(k, carry):
            to = partner(me, k)
            pltpu.make_async_remote_copy(
                src.at[fs, :, pl.ds(pl.multiple_of(PLANES * to, PLANES), PLANES)],
                dst.at[z, quarter, fs], sem.at[g], recv.at[g],
                device_id=(seg, to), device_id_type=MESH,
            ).start()
            return carry

        lax.fori_loop(k0, k1, body, 0)

    def return_res(g, k0, k1):
        scatter_back(res, res_in, sem_r, recv_r, g, k0, k1)

    def return_grad(g):
        scatter_back(grad, grad_in, sem_g, recv_g, g, 0, SLABS - 1)

    def keep_own(src, dst, g):
        f0, n = GROUPS[g]
        for f in range(f0, f0 + n):
            dst[z, quarter, f] = src[f, :, own, :]

    def face_values(k):
        halves = [vcol[j, at(k), :] for j in range(2)]
        found = neighbours(halves, [vhalo[d, packed(k), :] for d in range(4)])
        for j in range(2):
            for d in range(4):
                faces[d, j, at(k), :] = 0.5 * (halves[j] + found[j][d])

    def horizontal(buf, phase, f, k, halves):
        found = neighbours(halves, [halo[phase, d, f, packed(k), :] for d in range(4)])
        terms = []
        for j in range(2):
            v, (east, west, north, south) = halves[j], found[j]
            terms.append(
                faces[EAST, j, at(k), :] * (east - v)
                - faces[WEST, j, at(k), :] * (v - west)
                + faces[NORTH, j, at(k), :] * (north - v)
                - faces[SOUTH, j, at(k), :] * (v - south)
            )
        return terms

    def window(buf, f, j, k):
        return buf[f, j, pl.ds(pl.multiple_of(k * CHUNK, 8), CHUNK + 2 * PAD), :]

    def middle(win):
        return win[PAD : PAD + CHUNK]

    def slope(win):
        return win[PAD + 1 : PAD + 1 + CHUNK] - win[PAD - 1 : PAD - 1 + CHUNK]

    def lanes_of(j):
        return slice(j * NX, (j + 1) * NX)

    def fields(g):
        f0, n = GROUPS[g]
        return range(f0, f0 + n)

    def explicit(buf, phase, g):
        def body(k):
            for f in fields(g):
                wins = [window(buf, f, j, k) for j in range(2)]
                halves = [middle(win) for win in wins]
                terms = horizontal(buf, phase, f, k, halves)
                for j in range(2):
                    term = terms[j] - buf[2, j, at(k, PAD), :] * slope(wins[j])
                    if f >= 2:
                        term = term + buf[5 - f, j, at(k, PAD), :]
                    work[f, at(k), lanes_of(j)] = halves[j] + DT * term

        over_chunks(body)

    def adjoint(state, buf, phase, g, minus=None, into=None):
        def body(k):
            for f in fields(g):
                wins = [window(buf, f, j, k) for j in range(2)]
                halves = [middle(win) for win in wins]
                terms = horizontal(buf, phase, f, k, halves)
                for j in range(2):
                    term = terms[j] + slope(window(state, 2, j, k) * wins[j])
                    if f >= 2:
                        term = term + buf[5 - f, j, at(k, PAD), :]
                    if f == 2:
                        total = None
                        for h in range(NF):
                            part = buf[h, j, at(k, PAD), :] * slope(window(state, h, j, k))
                            total = part if total is None else total + part
                        term = term - total
                    out = halves[j] + DT * term
                    if minus is None:
                        work[f, at(k), lanes_of(j)] = out
                    else:
                        into[f, j, at(k), :] = out - minus[f, j, at(k), :]

        over_chunks(body)

    def product(matrix, f):
        return jnp.dot(
            matrix, work[f], precision=lax.Precision.HIGHEST, preferred_element_type=jnp.float32
        )

    def store(buf, f, value):
        for j in range(2):
            buf[f, j, PAD : PAD + NZ, :] = value[:, lanes_of(j)]

    def stage_first(g):
        wait_halo(0, g)
        explicit(q, 0, g)
        for f in fields(g):
            store(first, f, product(inv[f], f))
        start_halo(first, 1, g)

    def stage_residual(g):
        wait_halo(1, g)
        explicit(first, 1, g)
        wait_target(g, recv_t)
        for f in fields(g):
            end = product(inv[f], f)
            for j in range(2):
                gap = end[:, lanes_of(j)] - target[f, j]
                res[f, j] = gap
                work[f, :, lanes_of(j)] = gap
            store(adj1, f, product(inv_t[f], f))
        start_halo(adj1, 2, g)
        prior_copy(g).start()

    def stage_back(g):
        wait_halo(2, g)
        adjoint(first, adj1, 2, g)
        for f in fields(g):
            store(adj2, f, product(inv_t[f], f))
        start_halo(adj2, 3, g)

    def stage_gradient(g):
        wait_halo(3, g)
        prior_copy(g).wait_recv()
        adjoint(q, adj2, 3, g, minus=prior, into=grad)

    some = pl.ds(0, PLANES * (SLABS - 1))
    last = SLABS - 1
    forward_target(0)
    start_halo(q, 0, 0)
    scatter_states(1, 10, 16)
    for share in shares:
        share.wait_recv()
    for xs in range(4):
        for zs in range(8):
            plane = PLANES * (zs * 4 + ((xs // 2 + zs) % 2) * 2 + xs % 2)
            for j in range(2):
                vcol[j, plane : plane + PLANES, :] = vset[xs, zs, j]
    over_chunks(pack_visc)
    for copy in visc_copies():
        copy.start()
    scatter_states(1, 16, 27)
    for copy in visc_copies():
        copy.wait_recv()
    over_chunks(face_values)
    stage_first(0)
    scatter_states(1, 27, last)
    stage_residual(0)
    return_res(0, 0, 8)
    forward_target(1)
    start_halo(q, 0, 1)
    return_res(0, 8, 20)
    stage_first(1)
    return_res(0, 20, last)
    stage_residual(1)
    return_res(1, 0, 10)
    stage_back(0)
    return_res(1, 10, 20)
    stage_back(1)
    return_res(1, 20, last)
    stage_gradient(0)
    return_grad(0)
    stage_gradient(1)
    return_grad(1)
    for g in range(2):
        keep_own(res, res_in, g)
        keep_own(grad, grad_in, g)

    def collect(recv, src, dst, g):
        f0, n = GROUPS[g]
        wait_many(res.at[pl.ds(f0, n), :, some], recv.at[g])
        for f in fields(g):
            unpack(src, dst, f)

    for g in range(2):
        collect(recv_r, res_in, res_out, g)
    for g in range(2):
        collect(recv_g, grad_in, grad_out, g)

    @pl.when(giver)
    def _():
        wait_many(send_v.at[pl.ds(0, 7)], sem_v)
        wait_many(send_v.at[0, pl.ds(0, 3)], sem_v)

    for copy in shares + visc_copies():
        copy.wait_send()
    for g in range(2):
        fs = pl.ds(GROUPS[g][0], GROUPS[g][1])
        wait_many(q.at[fs, :, some], sem_q.at[g])
        for phase in range(4):
            for copy in halo_copies(phase, g):
                copy.wait_send()
        wait_target(g, sem_t)
        prior_copy(g).wait_send()
        for sem in (sem_r, sem_g):
            wait_many(res.at[fs, :, some], sem.at[g])


def finish_kernel(res_in, grad_in, res_out, grad_out, sem):
    rows = NF * PLANES * NY // 2
    copies = [
        pltpu.make_async_copy(src.at[pl.ds(i * rows, rows)], dst.at[pl.ds(i * rows, rows)], sem.at[n, i])
        for n, (src, dst) in enumerate(((res_in, res_out), (grad_in, grad_out)))
        for i in range(2)
    ]
    for copy in copies:
        copy.start()
    for copy in copies:
        copy.wait()


def local(states, viscosity, inverse):
    vmem = pl.BlockSpec(memory_space=pltpu.VMEM)
    hbm = pl.BlockSpec(memory_space=pltpu.MemorySpace.HBM)
    f32 = jnp.float32
    sem = pltpu.SemaphoreType.DMA
    flat = jax.ShapeDtypeStruct((NF * PLANES * NY, NX), f32)
    spread = pltpu.VMEM((8, 4, NF, 2, PLANES, NX), f32)
    padded = pltpu.VMEM((NF, 2, NZ + 2 * PAD, NX), f32)
    column = pltpu.VMEM((NF, 2, NZ, NX), f32)
    sems = [sem((3,)), sem((4, 2, 4)), sem((4,)), sem((2,)), sem((2,)), sem((2,)), sem((2,))]
    packed = 8 * CHUNKS
    res, grad = pl.pallas_call(
        orbit_kernel,
        out_shape=(flat, flat),
        in_specs=[hbm] * 3,
        out_specs=(vmem, vmem),
        scratch_shapes=[
            pltpu.VMEM((NF * PLANES * NY, NX), f32),
            pltpu.VMEM((PLANES * NY, NX), f32),
            pltpu.VMEM((NF, NZ, NZ), f32),
            spread,
            pltpu.VMEM((8, 4, 2, PLANES, NX), f32),
            padded, padded, padded, padded,
            column, column, column, column,
            pltpu.VMEM((4, 8, 2, PLANES, NX), f32),
            pltpu.VMEM((2, NZ, NX), f32),
            pltpu.VMEM((4, 2, NZ, NX), f32),
            pltpu.VMEM((NF, NZ, 2 * NX), f32),
            pltpu.VMEM((NF, NZ, NZ), f32),
            pltpu.VMEM((4, 4, NF, packed, NX), f32),
            pltpu.VMEM((4, 4, NF, packed, NX), f32),
            pltpu.VMEM((4, packed, NX), f32),
            pltpu.VMEM((4, packed, NX), f32),
            spread, spread, sem((4,)), sem((2, 8)), sem, *sems, sem((2,)), sem, *sems,
        ],
        compiler_params=pltpu.CompilerParams(
            collective_id=0, has_side_effects=True, vmem_limit_bytes=48 << 20
        ),
        name="orbit",
    )(
        *(
            pltpu.with_memory_space_constraint(value, pltpu.MemorySpace.HBM)
            for value in (
                states.reshape(NF * PLANES * NY, NX), viscosity.reshape(PLANES * NY, NX), inverse
            )
        )
    )
    res, grad = pl.pallas_call(
        finish_kernel,
        out_shape=(flat, flat),
        in_specs=[vmem] * 2,
        out_specs=(hbm, hbm),
        scratch_shapes=[sem((2, 2))],
        compiler_params=pltpu.CompilerParams(vmem_limit_bytes=16 << 20),
        name="finish",
    )(res, grad)
    shape = (1, NF, PLANES, NY, NX)
    return res.reshape(shape), grad.reshape(shape)


def solution(mesh):
    spec = P("seg", None, "slab", None, None)
    return jax.shard_map(
        local,
        mesh=mesh,
        in_specs=(spec, P("slab", None, None), P()),
        out_specs=(spec, spec),
        check_vma=False,
    )
```
